512 devices in a mesh: ep: 128 (over z, y, core), tp: 4 (over x).
Axes of the slice: x: 4, y: 8, z: 8, core: 2. Of those that a mesh axis runs over, the one named last changes fastest.
Arguments:
- grad_out: bfloat16 [16384, 3584], P('ep', 'tp'), may hold values from -6 to 6
- routes: int32 [16384, 8], P('ep'), may hold values from 0 to 127, all different within a row; in each aligned block of 128 rows (0 to 127, 128 to 255, ...) at most 10 rows name the same one
- gate_weights: float32 [16384, 8], P('ep'), may hold values from 0.05 to 0.5
- gate_act: bfloat16 [128, 1280, 1024], P('ep', None, 'tp'), may hold values from -6 to 6
- w_down: bfloat16 [128, 1024, 3584], P('ep', None, 'tp'), may hold values from -0.1875 to 0.1875
- w_up: bfloat16 [128, 3584, 1024], P('ep', 'tp'), may hold values from -0.09375 to 0.09375
Outputs:
- grad_in: bfloat16 [16384, 3584], P('ep', 'tp')
The draws below stay inside these ranges and needn't reach their ends.
Inputs may be any that keep to these rules, and one draw needn't show every extreme that they name: `routes`: each row names 8 different experts; among the 128 rows of one device no expert is named more than 10 times, a bound that some block reaches.
All inputs are finite; a program needn't handle non-finite values.
Results may differ from the reference program's by a relative error of at most 0.02.
Values may be sent and summed in bfloat16 or wider, within the bound.
A program may use at most 64 MiB of HBM per device.

```python
import math
import jax
import jax.numpy as jnp
import numpy as np
from jax import lax

D = 3584
F = 1024
TOP = 8
TOK_DEV = 128
EXPERTS = 128
SLOT = 10
ROWS = 1280
TOKENS = 16384
N_EP = 128
N_TP = 4


def levels(rng, dims, pieces, smallest, high):
    level, own = 1.0, jax.random.fold_in(rng, 6)
    for dim, shards_of in pieces:
        heights = jnp.exp(jax.random.uniform(jax.random.fold_in(own, dim), (shards_of,), jnp.float32, smallest / len(pieces), high / len(pieces)))
        level = level * jnp.repeat(heights, dims[dim] // shards_of).reshape([-1 if axis == dim else 1 for axis in range(len(dims))])
    return level


def deal_out(own_key, own, number, rows, amount, top, limit, skew):
    ranking = jax.random.permutation(own_key, amount)
    packed, common = portions_of(amount, rows * top, limit, skew, True), portions_of(amount, rows * top, limit, skew, False)
    places = jnp.arange(amount)

    def named(tallies, offset_by):
        used = int((tallies > 0).sum())
        fixed = max(1, used // 4)
        passed = fixed + (places - fixed + offset_by * (used - fixed)) % max(1, amount - fixed)
        return jnp.zeros((amount,), jnp.int32).at[ranking[jnp.where(places < fixed, places, passed)]].set(jnp.asarray(tallies, jnp.int32))

    tallies = jnp.where(number % 4 == 0, named(packed, number // 4), named(common, number - number // 4 - 1))
    mixed = jax.random.permutation(jax.random.fold_in(own, 3), amount)
    source_of, receiver = mixed[0:amount // 2 * 2:2], mixed[1:amount // 2 * 2:2]
    slack = jnp.minimum(tallies[source_of] - 1, limit - tallies[receiver]) // 2
    slack = jnp.where((source_of == ranking[0]) | (receiver == ranking[0]) | (tallies[receiver] == 0), 0, jnp.maximum(slack, 0))
    passed = jax.random.randint(jax.random.fold_in(own, 4), (amount // 2,), 0, 1 << 20) % (slack + 1)
    tallies = tallies.at[source_of].add(-passed).at[receiver].add(passed)
    items = jnp.searchsorted(jnp.cumsum(tallies), jnp.arange(rows * top), side="right").astype(jnp.int32)
    table = items.reshape(top, rows).T
    table = table[jax.random.permutation(jax.random.fold_in(own, 1), rows)]
    offset_by = jax.random.randint(jax.random.fold_in(own, 2), (rows, 1), 0, top)
    return jnp.take_along_axis(table, (jnp.arange(top)[None, :] + offset_by) % top, axis=1)


def portions_of(count, total, limit, lean, full):
    portions = [(1 << 20) // math.isqrt(rank ** lean) + 1 for rank in range(1, count + 1)]
    largest = limit if full else min(limit, max(-(-total // count), total * portions[0] // sum(portions)))
    least = 1 if total - largest >= count - 1 else 0
    counts, spare = [largest] + [least] * (count - 1), total - largest - least * (count - 1)
    while spare > 0:
        movable = [i for i in range(1, count) if counts[i] < largest] or [i for i in range(1, count) if counts[i] < limit]
        pool, remaining = sum([portions[i] for i in movable]), spare
        for i in movable:
            more = min(limit - counts[i], max(1, remaining * portions[i] // pool), spare)
            counts[i] = counts[i] + more
            spare = spare - more
    return np.array(counts)


def centred(rng, shape, width, bound, shards=(), held_as=jnp.bfloat16):
    factor_of = levels(rng, shape, shards, -0.22, 0.18) if shards else 1.0
    values = jax.random.normal(rng, shape, jnp.float32) * width * factor_of
    return jnp.minimum(jnp.maximum(values, -bound), bound).astype(held_as)


def setup_inputs(seed: int = 0) -> dict:
    splits = jax.random.split(jax.random.key(seed), 7)
    grad_out = centred(splits[0], (TOKENS, D), 1.0, 6.0, ((0, 128), (1, 4)))
    routes_keys = jax.random.split(jax.random.fold_in(splits[1], 1), TOKENS // TOK_DEV)
    routes_turns = jax.random.permutation(jax.random.fold_in(splits[1], 3), TOKENS // TOK_DEV)
    routes = jax.vmap(lambda own, number: deal_out(jax.random.fold_in(splits[1], 2), own, number, TOK_DEV, EXPERTS, TOP, SLOT, 2))(routes_keys, routes_turns).reshape((TOKENS, TOP))
    gate_weights = jnp.clip(jnp.exp(math.log(0.5) - 2.3025851 * jax.random.uniform(splits[2], (TOKENS, TOP), jnp.float32) ** levels(splits[2], (TOKENS, TOP), ((0, 128),), -0.2, 0.2)), 0.05, 0.5)
    gate_act = centred(splits[3], (EXPERTS, ROWS, F), 1.0, 6.0, ((0, 128), (2, 4)))
    w_down = centred(splits[4], (EXPERTS, F, D), F ** -0.5, 0.1875, ((0, 128), (2, 4)))
    w_up = centred(splits[5], (EXPERTS, D, F), D ** -0.5, 0.09375, ((0, 128), (1, 4)))
    return {"grad_out": grad_out, "routes": routes, "gate_weights": gate_weights, "gate_act": gate_act, "w_down": w_down, "w_up": w_up}


def reference(grad_out, routes, gate_weights, gate_act, w_down, w_up):
    source_dev = (jnp.arange(TOKENS, dtype=jnp.int32) // TOK_DEV).astype(jnp.int32)
    flat_ids = routes.reshape(N_EP, TOK_DEV * TOP)
    one_hot = (flat_ids[:, :, None] == jnp.arange(EXPERTS, dtype=jnp.int32)[None, None, :]).astype(jnp.int32)
    earlier = jnp.cumsum(one_hot, axis=1) - one_hot
    slot_rank = jnp.sum(earlier * one_hot, axis=2).reshape(TOKENS, TOP).astype(jnp.int32)
    position = (routes * ROWS + source_dev[:, None] * SLOT + slot_rank).astype(jnp.int32).reshape(-1)
    token_ids = jnp.repeat(jnp.arange(TOKENS, dtype=jnp.int32), TOP)
    token_of = jnp.full((EXPERTS * ROWS,), TOKENS, jnp.int32).at[position].set(token_ids)
    weight_of = jnp.zeros((EXPERTS * ROWS,), jnp.float32).at[position].set(gate_weights.reshape(-1).astype(jnp.float32))
    padded = jnp.concatenate([grad_out, jnp.zeros((1, D), grad_out.dtype)], axis=0)
    token_of = token_of.reshape(EXPERTS, ROWS)
    weight_of = weight_of.reshape(EXPERTS, ROWS)
    quarter = D // N_TP

    def one_expert(accum, inputs):
        token_row, weight_row, act_row, down_mat, up_mat = inputs
        routed = (padded[token_row].astype(jnp.float32) * weight_row[:, None]).astype(jnp.bfloat16)
        hidden_grad = jnp.zeros((ROWS, F), jnp.float32)
        for part in range(N_TP):
            lower = part * quarter
            term = jnp.dot(routed[:, lower:lower + quarter], down_mat[:, lower:lower + quarter].T, preferred_element_type=jnp.float32)
            hidden_grad = hidden_grad + term.astype(jnp.bfloat16).astype(jnp.float32)
        up_grad = (hidden_grad * act_row.astype(jnp.float32)).astype(jnp.bfloat16)
        row_grad = jnp.dot(up_grad, up_mat.T, preferred_element_type=jnp.float32).astype(jnp.bfloat16)
        accum = accum.at[token_row].add(row_grad.astype(jnp.float32))
        return accum, None

    start = jnp.zeros((TOKENS + 1, D), jnp.float32)
    accum, _ = lax.scan(one_expert, start, (token_of, weight_of, gate_act, w_down, w_up))
    return accum[:TOKENS].astype(jnp.bfloat16)
```

```python
import functools

import jax
import jax.numpy as jnp
from jax import lax
from jax.experimental import pallas as pl
from jax.experimental.pallas import tpu as pltpu
from jax.sharding import PartitionSpec as P

MESH = pl.DeviceIdType.MESH
RING = 8
SLOT = 10
CHUNKS = 8
FIRST = 3
NEAR = (0, 1, 7, 2, 6, 3, 5, 4)
PLACE = {offset: place for place, offset in enumerate(NEAR)}
GATHER_AHEAD = 3
COMBINE_LAG = 6
BF16 = jnp.bfloat16
F32 = jnp.float32
ABT = (((1,), (1,)), ((), ()))
ATB = (((0,), (0,)), ((), ()))


def hop_of(chunk):
    return lax.rem(chunk * 3 + FIRST, RING)


def on_core(
    grad_ref, ids_ref, gates_ref, act_hbm, down_hbm, up_hbm, out_ref,
    act, down, up, act_rows, meta_out, meta, tokens, picks, to_expert, routed,
    hidden, relay, passed, arrived, wide, row_grad, returned, totals, sum_out, sum_in,
    load_sem, a_send, a_recv, m_send, m_recv, b_send, b_recv, r_send, r_recv,
    p_send, p_recv, g_send, g_recv, f_send, f_recv, y_send, y_recv, s_send, s_recv,
):
    token_n, feat = grad_ref.shape
    half_tok = token_n // 2
    msg = RING * SLOT
    ep, tp = lax.axis_index("ep"), lax.axis_index("tp")
    tp_n = lax.axis_size("tp")
    core = lax.rem(ep, 2)
    y = lax.rem(ep // 2, RING)
    z = ep // (2 * RING)
    a = z * (1 - core) + y * core
    b = y * (1 - core) + z * core

    def device(a_at, b_at, role, core_at):
        return (a_at * (RING - (RING - 1) * role) + b_at * (1 + (RING - 1) * role)) * 2 + core_at

    def ring(value):
        return lax.rem(value + 2 * RING, RING)

    right, left = lax.rem(tp + 1, tp_n), lax.rem(tp + tp_n - 1, tp_n)
    across = lax.rem(tp + 2, tp_n)

    barrier = pltpu.get_barrier_semaphore()
    for other in range(2):
        for step in range(RING):
            for z_at, y_at in ((ring(z + step), y), (z, ring(y + step)))[: 1 if step == 0 else 2]:
                peer = (z_at * RING + y_at) * 2 + lax.rem(core + other, 2)
                if step or other:
                    pl.semaphore_signal(barrier, inc=1, device_id=(peer, tp), device_id_type=MESH)
    for peer in (right, left):
        pl.semaphore_signal(barrier, inc=1, device_id=(ep, peer), device_id_type=MESH)

    loads = [
        pltpu.make_async_copy(src, dst, load_sem.at[i])
        for i, (src, dst) in enumerate(((act_hbm, act), (down_hbm, down), (up_hbm, up)))
    ]
    for load in loads:
        load.start()

    def remote(src, dst, send, recv, to):
        return pltpu.make_async_remote_copy(
            src_ref=src, dst_ref=dst, send_sem=send, recv_sem=recv, device_id=to, device_id_type=MESH
        )

    def arrival(ref, sem):
        pltpu.make_async_copy(ref, ref, sem).wait()

    shape = (token_n, token_n)
    row = lax.broadcasted_iota(jnp.int32, shape, 0)
    chunk_of, core_of = (row >> 1) & 7, row & 1
    a_of = (row // 16 + a) & 7
    b_of = (chunk_of * 3 + FIRST + b) & 7
    expert = a_of * (16 - 14 * core) + b_of * (2 + 14 * core) + core_of
    named = jnp.zeros(shape, F32)
    weight = jnp.zeros(shape, F32)
    for k in range(ids_ref.shape[0]):
        hit = expert == ids_ref[k : k + 1, :]
        named = jnp.where(hit, 1.0, named)
        weight = jnp.where(hit, gates_ref[k : k + 1, :], weight)
    before = (row < lax.broadcasted_iota(jnp.int32, shape, 1)).astype(BF16)
    rank = jnp.dot(named.astype(BF16), before, preferred_element_type=F32)
    slot = jnp.where(named > 0.0, rank, -1000.0)
    for m in range(RING):
        meta_out[m, 0:16, :] = slot[m * 16 : (m + 1) * 16, :]
        meta_out[m, 16:32, :] = weight[m * 16 : (m + 1) * 16, :]
    meta[0] = meta_out[0]
    tokens[0] = grad_ref[...]
    totals[...] = jnp.zeros(totals.shape, F32)

    pl.semaphore_wait(barrier, 4 * (RING - 1) + 1 + 2)

    steps_of = ((4, 3), (3, 4))
    a_next = (device(ring(a + 1), b, core, core), device(ring(a - 1), b, core, core))

    def spread(way, h, s):
        rows = pl.ds(h * half_tok, half_tok)
        src_off, dst_off = ((RING - s) % RING, RING - 1 - s) if way == 0 else (s, s + 1)
        src = grad_ref.at[rows] if s == 0 else tokens.at[PLACE[src_off], rows]
        at = (way * 2 + h) * 4 + s
        return remote(
            src, tokens.at[PLACE[dst_off], rows], a_send.at[at], a_recv.at[at], (a_next[way], tp)
        )

    metas = [
        remote(
            meta_out.at[m], meta.at[PLACE[RING - m]], m_send.at[m], m_recv.at[RING - m],
            (device(ring(a + m), b, core, core), tp),
        )
        for m in range(1, RING)
    ]
    for copy in metas:
        copy.start()

    act_n = act.shape[0]
    wide_shape = (2 * msg, 128)
    row = lax.broadcasted_iota(jnp.int32, wide_shape, 0)
    lane = lax.broadcasted_iota(jnp.int32, wide_shape, 1)
    from_one = row >= msg
    inner = jnp.where(from_one, row - msg, row)
    offset = jnp.full(wide_shape, NEAR[0], jnp.int32)
    in_slot = inner
    for place in range(1, RING):
        past = inner >= place * SLOT
        offset = jnp.where(past, NEAR[place], offset)
        in_slot = jnp.where(past, inner - place * SLOT, in_slot)
    act_base = in_slot + jnp.where(
        from_one,
        ((offset + y) & 7) * (2 * SLOT) + SLOT,
        ((offset + z) & 7) * (2 * SLOT * RING),
    )

    def order_act(k, carry):
        hop = hop_of(k)
        natural = act_base + jnp.where(
            from_one, ring(z - hop) * (2 * SLOT * RING), ring(y - hop) * (2 * SLOT)
        )
        pick = jnp.concatenate(
            [(lane + i * 128 == natural).astype(F32).astype(BF16) for i in range(act_n // 128)], axis=1
        )
        got = jnp.dot(pick, act[...], preferred_element_type=F32).astype(BF16)
        act_rows[k] = got.reshape(act_rows.shape[1:])
        return carry

    for s in range(4):
        for h in range(2):
            for way in range(2):
                if s < steps_of[way][h]:
                    if s:
                        spread(way, h, s - 1).wait_recv()
                    spread(way, h, s).start()
        if s == 0:
            loads[0].wait()
        lax.fori_loop(s * 2, s * 2 + 2, order_act, 0)
    for way in range(2):
        for h in range(2):
            spread(way, h, steps_of[way][h] - 1).wait_recv()
    for m in range(1, RING):
        metas[m - 1].wait_recv()
    loads[1].wait()
    loads[2].wait()

    msg_row = lax.broadcasted_iota(jnp.int32, (msg, token_n), 0).astype(F32)

    def gather(k):
        hop = hop_of(k)
        gates = []
        for c in range(2):
            gate = jnp.zeros((msg, token_n), F32)
            for place in range(RING):
                at = meta[place, pl.ds(k * 2 + c, 1), :] + float(place * SLOT)
                hit = msg_row == at
                gate = jnp.where(hit, meta[place, pl.ds(16 + k * 2 + c, 1), :], gate)
                picks[k, c * msg : (c + 1) * msg, place * token_n : (place + 1) * token_n] = (
                    jnp.where(hit, 1.0, 0.0).astype(BF16)
                )
            gates.append(jnp.sum(gate, axis=1, keepdims=True))
        rows = jnp.dot(
            picks[k], tokens[...].reshape(RING * token_n, feat), preferred_element_type=F32
        )
        for c in range(2):
            to_expert[k, c] = (rows[c * msg : (c + 1) * msg] * gates[c]).astype(BF16)
        for c in range(2):
            here = jnp.logical_and(hop == 0, core == c)

            @pl.when(here)
            def _():
                pltpu.make_async_copy(to_expert.at[k, c], routed.at[k, core], b_recv.at[k, core]).start()

            @pl.when(jnp.logical_not(here))
            def _():
                remote(
                    to_expert.at[k, c], routed.at[k, core], b_send.at[k, c], b_recv.at[k, core],
                    (device(a, ring(b + hop), core, c), tp),
                ).start()

    def r_copy(k, i):
        src, dst, to = (
            (hidden.at[k, across, 0], relay.at[k, 0], right),
            (hidden.at[k, right, 1], arrived.at[k, 0, 1], right),
            (hidden.at[k, across, 1], relay.at[k, 1], left),
            (hidden.at[k, left, 0], arrived.at[k, 1, 0], left),
        )[i]
        return remote(src, dst, r_send.at[k, i], r_recv.at[k, i], (ep, to))

    def p_copy(k, way):
        dst, to = ((arrived.at[k, 0, 0], right), (arrived.at[k, 1, 1], left))[way]
        return remote(passed.at[k, way], dst, p_send.at[k, way], p_recv.at[k, way], (ep, to))

    def g_copy(k, way):
        return remote(
            wide.at[k, tp], wide.at[k, tp], g_send.at[k, way], g_recv.at[k, way],
            (ep, (right, left)[way]),
        )

    def f_copy(k, way):
        part = wide.at[k, (left, right)[way], way]
        return remote(part, part, f_send.at[k, way], f_recv.at[k, way], (ep, (right, left)[way]))

    def project_down(k):
        for c in range(2):
            arrival(routed.at[k, c], b_recv.at[k, c])
        rows = routed[k].reshape(2 * msg, feat)
        part = hidden.shape[-1]
        for q in range(hidden.shape[1]):
            value = lax.dot_general(
                rows, down[q * part : (q + 1) * part, :], ABT, preferred_element_type=F32
            )
            hidden[k, q] = value.astype(BF16).reshape(2, msg, part)
        for i in (0, 2, 1, 3):
            r_copy(k, i).start()

    def pass_on(k):
        for way, to in ((0, right), (1, left)):
            r_copy(k, way * 2).wait_recv()
            passed[k, way] = (
                hidden[k, to, way].astype(F32) + relay[k, way].astype(F32)
            ).astype(BF16)
            p_copy(k, way).start()

    def finish_hidden(k):
        r_copy(k, 1).wait_recv()
        r_copy(k, 3).wait_recv()
        p_copy(k, 0).wait_recv()
        p_copy(k, 1).wait_recv()
        value = hidden[k, tp].astype(F32) + (
            arrived[k, 0].astype(F32) + arrived[k, 1].astype(F32)
        )
        wide[k, tp] = (value * act_rows[k].astype(F32)).astype(BF16)
        for way in range(2):
            g_copy(k, way).start()

    def hand_over(k):
        for way in range(2):
            arrival(wide.at[k, (left, right)[way]], g_recv.at[k, way])
            f_copy(k, way).start()

    def project_up(k):
        for way in range(2):
            arrival(wide.at[k, across, way], f_recv.at[k, way])
        part = wide.shape[-1]
        rows = jnp.concatenate(
            [wide[k, q].reshape(2 * msg, part) for q in range(wide.shape[1])], axis=1
        )
        value = lax.dot_general(rows, up[...], ABT, preferred_element_type=F32).astype(BF16)
        row_grad[k] = value.reshape(2, msg, feat)
        hop = hop_of(k)
        for c in range(2):
            here = jnp.logical_and(hop == 0, core == c)
            to = device(z, ring(y - hop), 0, 0) if c == 0 else device(y, ring(z - hop), 1, 1)

            @pl.when(here)
            def _():
                pltpu.make_async_copy(row_grad.at[k, c], returned.at[k, core], y_recv.at[k, core]).start()

            @pl.when(jnp.logical_not(here))
            def _():
                remote(
                    row_grad.at[k, c], returned.at[k, core], y_send.at[k, c], y_recv.at[k, core],
                    (to, tp),
                ).start()

    def combine(k):
        for c in range(2):
            arrival(returned.at[k, c], y_recv.at[k, c])
        rows = returned[k].reshape(2 * msg, feat)
        value = lax.dot_general(picks[k], rows, ATB, preferred_element_type=F32)
        totals[...] += value.reshape(totals.shape)

    def first(k, carry):
        gather(k)
        return carry

    lax.fori_loop(0, GATHER_AHEAD, first, 0)

    stages = (
        (project_down, 0),
        (pass_on, 1),
        (finish_hidden, 2),
        (hand_over, 3),
        (project_up, 4),
        (combine, COMBINE_LAG),
    )

    def turn(t, carry):
        for stage, lag in stages:

            @pl.when(jnp.logical_and(t >= lag, t < lag + CHUNKS))
            def _():
                stage(t - lag)

            if lag == 0:

                @pl.when(t < CHUNKS - GATHER_AHEAD)
                def _():
                    gather(t + GATHER_AHEAD)

        return carry

    lax.fori_loop(0, CHUNKS + COMBINE_LAG, turn, 0)

    chain_of = (((4, 3, 2, 1), (3, 2, 1)), ((5, 6, 7), (4, 5, 6, 7)))

    def sum_copy(way, h, s):
        at = (way * 2 + h) * 4 + s
        return remote(
            sum_out.at[way, h, s], sum_in.at[way, h, s], s_send.at[at], s_recv.at[at],
            (a_next[way], tp),
        )

    for s in range(4):
        for h, way in ((0, 0), (1, 1), (1, 0), (0, 1)):
            chain = chain_of[way][h]
            if s < len(chain):
                value = totals[PLACE[chain[s]], h * half_tok : (h + 1) * half_tok, :]
                if s:
                    sum_copy(way, h, s - 1).wait_recv()
                    value = value + sum_in[way, h, s - 1].astype(F32)
                sum_out[way, h, s] = value.astype(BF16)
                sum_copy(way, h, s).start()
    for h in range(2):
        value = totals[0, h * half_tok : (h + 1) * half_tok, :]
        for way in range(2):
            last = len(chain_of[way][h]) - 1
            sum_copy(way, h, last).wait_recv()
            value = value + sum_in[way, h, last].astype(F32)
        out_ref[h * half_tok : (h + 1) * half_tok, :] = value.astype(BF16)

    for copy in metas:
        copy.wait_send()
    for way in range(2):
        for h in range(2):
            for s in range(steps_of[way][h]):
                spread(way, h, s).wait_send()
                sum_copy(way, h, s).wait_send()

    def drain(k, carry):
        hop = hop_of(k)
        for c in range(2):

            @pl.when(jnp.logical_not(jnp.logical_and(hop == 0, core == c)))
            def _():
                arrival(to_expert.at[k, c], b_send.at[k, c])
                arrival(row_grad.at[k, c], y_send.at[k, c])

        for i in range(4):
            r_copy(k, i).wait_send()
        for way in range(2):
            p_copy(k, way).wait_send()
            g_copy(k, way).wait_send()
            f_copy(k, way).wait_send()
        return carry

    lax.fori_loop(0, CHUNKS, drain, 0)


def on_device(grad_out, routes, gate_weights, gate_act, w_down, w_up):
    token_n, feat = grad_out.shape
    act, down, up = gate_act[0], w_down[0], w_up[0]
    hid_n = down.shape[0]
    hid = act.shape[1]
    tp_n = hid_n // hid
    msg = RING * SLOT
    half = token_n // 2
    dma = pltpu.SemaphoreType.DMA
    vmem = pl.BlockSpec(memory_space=pltpu.VMEM)
    hbm = pl.BlockSpec(memory_space=pl.ANY)
    return pl.pallas_call(
        on_core,
        out_shape=jax.ShapeDtypeStruct((token_n, feat), BF16),
        in_specs=[vmem, vmem, vmem, hbm, hbm, hbm],
        out_specs=vmem,
        scratch_shapes=[
            pltpu.VMEM(act.shape, BF16),
            pltpu.VMEM(down.shape, BF16),
            pltpu.VMEM(up.shape, BF16),
            pltpu.VMEM((CHUNKS, 2, msg, hid), BF16),
            pltpu.VMEM((RING, 32, token_n), F32),
            pltpu.VMEM((RING, 32, token_n), F32),
            pltpu.VMEM((RING, token_n, feat), BF16),
            pltpu.VMEM((CHUNKS, 2 * msg, RING * token_n), BF16),
            pltpu.VMEM((CHUNKS, 2, msg, feat), BF16),
            pltpu.VMEM((CHUNKS, 2, msg, feat), BF16),
            pltpu.VMEM((CHUNKS, tp_n, 2, msg, hid), BF16),
            pltpu.VMEM((CHUNKS, 2, msg, hid), BF16),
            pltpu.VMEM((CHUNKS, 2, msg, hid), BF16),
            pltpu.VMEM((CHUNKS, 2, 2, msg, hid), BF16),
            pltpu.VMEM((CHUNKS, tp_n, 2, msg, hid), BF16),
            pltpu.VMEM((CHUNKS, 2, msg, feat), BF16),
            pltpu.VMEM((CHUNKS, 2, msg, feat), BF16),
            pltpu.VMEM((RING, token_n, feat), F32),
            pltpu.VMEM((2, 2, 4, half, feat), BF16),
            pltpu.VMEM((2, 2, 4, half, feat), BF16),
            dma((3,)),
            dma((16,)), dma((16,)),
            dma((RING,)), dma((RING,)),
            dma((CHUNKS, 2)), dma((CHUNKS, 2)),
            dma((CHUNKS, 4)), dma((CHUNKS, 4)),
            dma((CHUNKS, 2)), dma((CHUNKS, 2)),
            dma((CHUNKS, 2)), dma((CHUNKS, 2)),
            dma((CHUNKS, 2)), dma((CHUNKS, 2)),
            dma((CHUNKS, 2)), dma((CHUNKS, 2)),
            dma((16,)), dma((16,)),
        ],
        compiler_params=pltpu.CompilerParams(
            collective_id=0, has_side_effects=True, vmem_limit_bytes=60 * 1024 * 1024
        ),
    )(grad_out, routes.T, gate_weights.T, act, down, up)


def solution(mesh):
    placed = (
        P("ep", "tp"),
        P("ep", None),
        P("ep", None),
        P("ep", None, "tp"),
        P("ep", None, "tp"),
        P("ep", "tp", None),
    )
    return jax.shard_map(
        on_device, mesh=mesh, in_specs=placed, out_specs=P("ep", "tp"), check_vma=False
    )
```

```python
import functools

import jax
import jax.numpy as jnp
from jax import lax
from jax.experimental import pallas as pl
from jax.experimental.pallas import tpu as pltpu
from jax.sharding import PartitionSpec as P

MESH = pl.DeviceIdType.MESH
RING = 8
SLOT = 10
GROUPS = 4
HOPS = (2, 6, 3, 5, 4, 0, 1, 7)
HOP_CODE = sum(hop << (3 * i) for i, hop in enumerate(HOPS))
PIECES = 4
WAVES = ((0, 48, 0, 5), (48, 32, 4, 4))
NEAR = (0, 1, 7, 2, 6, 3, 5, 4)
PLACE = {offset: place for place, offset in enumerate(NEAR)}
COMBINE_LAG = 6
BF16 = jnp.bfloat16
F32 = jnp.float32
ABT = (((1,), (1,)), ((), ()))
ATB = (((0,), (0,)), ((), ()))


def hop_of(i):
    return (HOP_CODE >> (3 * i)) & 7


def on_core(
    grad_ref, ids_ref, gates_ref, act_hbm, down_hbm, up_hbm, out_ref,
    act, down, up, meta_out, meta, tokens, totals, sum_out, sum_in, waves,
    load_sem, a_send, a_recv, m_send, m_recv, b_send, b_recv, r_send, r_recv,
    p_send, p_recv, g_send, g_recv, f_send, f_recv, y_send, y_recv, s_send, s_recv,
):
    token_n, feat = grad_ref.shape
    piece = token_n // PIECES
    ep, tp = lax.axis_index("ep"), lax.axis_index("tp")
    tp_n = lax.axis_size("tp")
    core = lax.rem(ep, 2)
    y = lax.rem(ep // 2, RING)
    z = ep // (2 * RING)
    a = z * (1 - core) + y * core
    b = y * (1 - core) + z * core

    def device(a_at, b_at, role, core_at):
        return (a_at * (RING - (RING - 1) * role) + b_at * (1 + (RING - 1) * role)) * 2 + core_at

    def ring(value):
        return lax.rem(value + 2 * RING, RING)

    right, left = lax.rem(tp + 1, tp_n), lax.rem(tp + tp_n - 1, tp_n)
    across = lax.rem(tp + 2, tp_n)

    barrier = pltpu.get_barrier_semaphore()
    for other in range(2):
        for step in range(RING):
            for z_at, y_at in ((ring(z + step), y), (z, ring(y + step)))[: 1 if step == 0 else 2]:
                peer = (z_at * RING + y_at) * 2 + lax.rem(core + other, 2)
                if step or other:
                    pl.semaphore_signal(barrier, inc=1, device_id=(peer, tp), device_id_type=MESH)
    for peer in (right, left):
        pl.semaphore_signal(barrier, inc=1, device_id=(ep, peer), device_id_type=MESH)

    loads = [
        pltpu.make_async_copy(src, dst, load_sem.at[i])
        for i, (src, dst) in enumerate(((act_hbm, act), (down_hbm, down), (up_hbm, up)))
    ]
    for load in loads:
        load.start()

    def remote(src, dst, send, recv, to):
        return pltpu.make_async_remote_copy(
            src_ref=src, dst_ref=dst, send_sem=send, recv_sem=recv, device_id=to, device_id_type=MESH
        )

    def arrival(ref, sem):
        pltpu.make_async_copy(ref, ref, sem).wait()

    shape = (token_n, token_n)
    row = lax.broadcasted_iota(jnp.int32, shape, 0)
    chunk_of, core_of = (row >> 1) & 7, row & 1
    a_of = (row // 16 + a) & 7
    b_of = (hop_of(chunk_of) + b) & 7
    expert = a_of * (16 - 14 * core) + b_of * (2 + 14 * core) + core_of
    named = jnp.zeros(shape, F32)
    weight = jnp.zeros(shape, F32)
    for k in range(ids_ref.shape[0]):
        hit = expert == ids_ref[k : k + 1, :]
        named = jnp.where(hit, 1.0, named)
        weight = jnp.where(hit, gates_ref[k : k + 1, :], weight)
    before = (row < lax.broadcasted_iota(jnp.int32, shape, 1)).astype(BF16)
    rank = jnp.dot(named.astype(BF16), before, preferred_element_type=F32)
    slot = jnp.where(named > 0.0, rank, -1000.0)
    for m in range(RING):
        meta_out[m, 0:16, :] = slot[m * 16 : (m + 1) * 16, :]
        meta_out[m, 16:32, :] = weight[m * 16 : (m + 1) * 16, :]
    meta[0] = meta_out[0]
    tokens[0] = grad_ref[...]
    totals[...] = jnp.zeros(totals.shape, F32)

    pl.semaphore_wait(barrier, 4 * (RING - 1) + 1 + 2)

    a_next = (device(ring(a + 1), b, core, core), device(ring(a - 1), b, core, core))

    def steps_of(way, p):
        return 4 if (p < PIECES // 2) == (way == 0) else 3

    turns = [
        (way, (i + way * PIECES // 2) % PIECES) for i in range(PIECES) for way in range(2)
    ]

    def spread(way, p, s):
        rows = pl.ds(p * piece, piece)
        src_off, dst_off = ((RING - s) % RING, RING - 1 - s) if way == 0 else (s, s + 1)
        src = grad_ref.at[rows] if s == 0 else tokens.at[PLACE[src_off], rows]
        at = (way * PIECES + p) * 4 + s
        return remote(
            src, tokens.at[PLACE[dst_off], rows], a_send.at[at], a_recv.at[at], (a_next[way], tp)
        )

    for way, p in turns:
        spread(way, p, 0).start()
    metas = [
        remote(
            meta_out.at[m], meta.at[PLACE[RING - m]], m_send.at[m], m_recv.at[RING - m],
            (device(ring(a + m), b, core, core), tp),
        )
        for m in range(1, RING)
    ]
    for copy in metas:
        copy.start()

    act_n = act.shape[0]

    def order_act(w):
        row0, rows, _, _ = WAVES[w]
        wide_shape = (4 * rows, 128)
        row = lax.broadcasted_iota(jnp.int32, wide_shape, 0)
        lane = lax.broadcasted_iota(jnp.int32, wide_shape, 1)
        later = row >= 2 * rows
        inner = jnp.where(later, row - 2 * rows, row)
        from_one = inner >= rows
        inner = jnp.where(from_one, inner - rows, inner) + row0
        offset = jnp.full(wide_shape, NEAR[0], jnp.int32)
        in_slot = inner
        for place in range(1, RING):
            past = inner >= place * SLOT
            offset = jnp.where(past, NEAR[place], offset)
            in_slot = jnp.where(past, inner - place * SLOT, in_slot)
        base = in_slot + jnp.where(
            from_one,
            ((offset + y) & 7) * (2 * SLOT) + SLOT,
            ((offset + z) & 7) * (2 * SLOT * RING),
        )

        def order(i, carry):
            hop = jnp.where(later, hop_of(2 * i + 1), hop_of(2 * i))
            natural = base + jnp.where(
                from_one,
                ((z - hop) & 7) * (2 * SLOT * RING),
                ((y - hop) & 7) * (2 * SLOT),
            )
            pick = jnp.concatenate(
                [(lane + j * 128 == natural).astype(F32).astype(BF16) for j in range(act_n // 128)],
                axis=1,
            )
            got = jnp.dot(pick, act[...], preferred_element_type=F32).astype(BF16)
            ordered = waves[w]["act"]
            ordered[i] = got.reshape(ordered.shape[1:])
            return carry

        return order

    order = [order_act(w) for w in range(2)]

    def gather(w, i):
        row0, rows, place0, places = WAVES[w]
        wave = waves[w]
        msg_row = lax.broadcasted_iota(jnp.int32, (rows, token_n), 0).astype(F32) + float(row0)
        gates = []
        for n in range(4):
            at_row = 4 * i + n
            gate = jnp.zeros((rows, token_n), F32)
            for p in range(places):
                place = place0 + p
                at = meta[place, pl.ds(at_row, 1), :] + float(place * SLOT)
                hit = msg_row == at
                gate = jnp.where(hit, meta[place, pl.ds(16 + at_row, 1), :], gate)
                wave["picks"][i, n * rows : (n + 1) * rows, p * token_n : (p + 1) * token_n] = (
                    jnp.where(hit, 1.0, 0.0).astype(BF16)
                )
            gates.append(jnp.sum(gate, axis=1, keepdims=True))
        source = tokens[place0 : place0 + places].reshape(places * token_n, feat)
        value = jnp.dot(wave["picks"][i], source, preferred_element_type=F32)
        for n in range(4):
            wave["to_expert"][i, n // 2, n % 2] = (
                value[n * rows : (n + 1) * rows] * gates[n]
            ).astype(BF16)
        g = w * GROUPS + i
        for n in range(4):
            kk, c = n // 2, n % 2
            hop = hop_of(2 * i + kk)
            here = jnp.logical_and(hop == 0, core == c)
            src, dst = wave["to_expert"].at[i, kk, c], wave["routed"].at[i, kk, core]

            @pl.when(here)
            def _():
                pltpu.make_async_copy(src, dst, b_recv.at[g, kk, core]).start()

            @pl.when(jnp.logical_not(here))
            def _():
                remote(
                    src, dst, b_send.at[g, kk, c], b_recv.at[g, kk, core],
                    (device(a, ring(b + hop), core, c), tp),
                ).start()

    def spread_step(s):
        for way, p in turns:
            if s < steps_of(way, p):
                spread(way, p, s - 1).wait_recv()
                spread(way, p, s).start()

    def early(i, carry):
        gather(0, i)
        return carry

    loads[0].wait()
    lax.fori_loop(0, 2, order[0], 0)
    spread_step(1)
    lax.fori_loop(2, GROUPS, order[0], 0)
    spread_step(2)
    for m in range(1, RING):
        metas[m - 1].wait_recv()
    lax.fori_loop(0, 2, early, 0)
    spread_step(3)
    lax.fori_loop(2, GROUPS, early, 0)
    loads[1].wait()
    loads[2].wait()

    def r_copy(w, i, n):
        hidden, relay, arrived = waves[w]["hidden"], waves[w]["relay"], waves[w]["arrived"]
        src, dst, to = (
            (hidden.at[i, across, 0], relay.at[i, 0], right),
            (hidden.at[i, right, 1], arrived.at[i, 0, 1], right),
            (hidden.at[i, across, 1], relay.at[i, 1], left),
            (hidden.at[i, left, 0], arrived.at[i, 1, 0], left),
        )[n]
        g = w * GROUPS + i
        return remote(src, dst, r_send.at[g, n], r_recv.at[g, n], (ep, to))

    def p_copy(w, i, way):
        arrived = waves[w]["arrived"]
        dst, to = ((arrived.at[i, 0, 0], right), (arrived.at[i, 1, 1], left))[way]
        g = w * GROUPS + i
        return remote(
            waves[w]["passed"].at[i, way], dst, p_send.at[g, way], p_recv.at[g, way], (ep, to)
        )

    def g_copy(w, i, way):
        part = waves[w]["wide"].at[i, tp]
        g = w * GROUPS + i
        return remote(part, part, g_send.at[g, way], g_recv.at[g, way], (ep, (right, left)[way]))

    def f_copy(w, i, way):
        part = waves[w]["wide"].at[i, (left, right)[way], way]
        g = w * GROUPS + i
        return remote(part, part, f_send.at[g, way], f_recv.at[g, way], (ep, (right, left)[way]))

    def project_down(w, i):
        wave, rows = waves[w], WAVES[w][1]
        for kk in range(2):
            for c in range(2):
                arrival(wave["routed"].at[i, kk, c], b_recv.at[w * GROUPS + i, kk, c])
        got = wave["routed"][i].reshape(4 * rows, feat)
        hidden = wave["hidden"]
        part = hidden.shape[-1]
        for q in range(hidden.shape[1]):
            value = lax.dot_general(
                got, down[q * part : (q + 1) * part, :], ABT, preferred_element_type=F32
            )
            hidden[i, q] = value.astype(BF16).reshape(2, 2 * rows, part)
        for n in (0, 2, 1, 3):
            r_copy(w, i, n).start()

    def pass_on(w, i):
        wave = waves[w]
        for way, to in ((0, right), (1, left)):
            r_copy(w, i, way * 2).wait_recv()
            wave["passed"][i, way] = (
                wave["hidden"][i, to, way].astype(F32) + wave["relay"][i, way].astype(F32)
            ).astype(BF16)
            p_copy(w, i, way).start()

    def finish_hidden(w, i):
        wave = waves[w]
        r_copy(w, i, 1).wait_recv()
        r_copy(w, i, 3).wait_recv()
        p_copy(w, i, 0).wait_recv()
        p_copy(w, i, 1).wait_recv()
        value = wave["hidden"][i, tp].astype(F32) + (
            wave["arrived"][i, 0].astype(F32) + wave["arrived"][i, 1].astype(F32)
        )
        wave["wide"][i, tp] = (value * wave["act"][i].astype(F32)).astype(BF16)
        for way in range(2):
            g_copy(w, i, way).start()

    def hand_over(w, i):
        for way in range(2):
            arrival(waves[w]["wide"].at[i, (left, right)[way]], g_recv.at[w * GROUPS + i, way])
            f_copy(w, i, way).start()

    def project_up(w, i):
        wave, rows = waves[w], WAVES[w][1]
        wide = wave["wide"]
        g = w * GROUPS + i
        for way in range(2):
            arrival(wide.at[i, across, way], f_recv.at[g, way])
        part = wide.shape[-1]
        got = jnp.concatenate(
            [wide[i, q].reshape(4 * rows, part) for q in range(wide.shape[1])], axis=1
        )
        value = lax.dot_general(got, up[...], ABT, preferred_element_type=F32).astype(BF16)
        wave["row_grad"][i] = value.reshape(2, 2, rows, feat)
        for n in range(4):
            kk, c = n // 2, n % 2
            hop = hop_of(2 * i + kk)
            here = jnp.logical_and(hop == 0, core == c)
            to = device(z, ring(y - hop), 0, 0) if c == 0 else device(y, ring(z - hop), 1, 1)
            src, dst = wave["row_grad"].at[i, kk, c], wave["returned"].at[i, kk, core]

            @pl.when(here)
            def _():
                pltpu.make_async_copy(src, dst, y_recv.at[g, kk, core]).start()

            @pl.when(jnp.logical_not(here))
            def _():
                remote(
                    src, dst, y_send.at[g, kk, c], y_recv.at[g, kk, core], (to, tp)
                ).start()

    def combine(w, i):
        _, rows, place0, places = WAVES[w]
        wave = waves[w]
        for kk in range(2):
            for c in range(2):
                arrival(wave["returned"].at[i, kk, c], y_recv.at[w * GROUPS + i, kk, c])
        got = wave["returned"][i].reshape(4 * rows, feat)
        value = lax.dot_general(wave["picks"][i], got, ATB, preferred_element_type=F32)
        totals[place0 : place0 + places] += value.reshape(places, token_n, feat)

    stages = (
        (project_down, 0),
        (pass_on, 1),
        (finish_hidden, 2),
        (hand_over, 3),
        (project_up, 4),
        (combine, COMBINE_LAG),
    )

    def turn(t, carry):
        for stage, lag in stages:
            for w in range(2):
                first = lag + w * GROUPS

                @pl.when(jnp.logical_and(t >= first, t < first + GROUPS))
                def _():
                    stage(w, t - first)

            if lag == 0:

                @pl.when(t == 0)
                def _():
                    for way, p in turns:
                        spread(way, p, steps_of(way, p) - 1).wait_recv()

                @pl.when(t < GROUPS)
                def _():
                    gather(1, t)
                    order[1](t, 0)

        return carry

    lax.fori_loop(0, 2 * GROUPS + COMBINE_LAG, turn, 0)

    def chain_of(way, p):
        chain = (4, 3, 2, 1) if way == 0 else (4, 5, 6, 7)
        return chain[4 - steps_of(way, p) :]

    def sum_copy(way, p, s):
        at = (way * PIECES + p) * 4 + s
        return remote(
            sum_out.at[way, p, s], sum_in.at[way, p, s], s_send.at[at], s_recv.at[at],
            (a_next[way], tp),
        )

    for s in range(4):
        for way, p in turns:
            chain = chain_of(way, p)
            if s < len(chain):
                value = totals[PLACE[chain[s]], p * piece : (p + 1) * piece, :]
                if s:
                    sum_copy(way, p, s - 1).wait_recv()
                    value = value + sum_in[way, p, s - 1].astype(F32)
                sum_out[way, p, s] = value.astype(BF16)
                sum_copy(way, p, s).start()
    for i in range(PIECES):
        p = (i + PIECES // 2) % PIECES
        value = totals[0, p * piece : (p + 1) * piece, :]
        for way in range(2):
            last = steps_of(way, p) - 1
            sum_copy(way, p, last).wait_recv()
            value = value + sum_in[way, p, last].astype(F32)
        out_ref[p * piece : (p + 1) * piece, :] = value.astype(BF16)

    for copy in metas:
        copy.wait_send()
    for way, p in turns:
        for s in range(steps_of(way, p)):
            spread(way, p, s).wait_send()
            sum_copy(way, p, s).wait_send()

    def drain(i, carry):
        for w in range(2):
            g = w * GROUPS + i
            for kk in range(2):
                hop = hop_of(2 * i + kk)
                for c in range(2):

                    @pl.when(jnp.logical_not(jnp.logical_and(hop == 0, core == c)))
                    def _():
                        arrival(waves[w]["to_expert"].at[i, kk, c], b_send.at[g, kk, c])
                        arrival(waves[w]["row_grad"].at[i, kk, c], y_send.at[g, kk, c])

            for n in range(4):
                r_copy(w, i, n).wait_send()
            for way in range(2):
                p_copy(w, i, way).wait_send()
                g_copy(w, i, way).wait_send()
                f_copy(w, i, way).wait_send()
        return carry

    lax.fori_loop(0, GROUPS, drain, 0)


def scratch_of(wave, token_n, feat, hid, tp_n):
    _, rows, _, places = wave
    shapes = {
        "act": (2, 2 * rows, hid),
        "picks": (4 * rows, places * token_n),
        "to_expert": (2, 2, rows, feat),
        "routed": (2, 2, rows, feat),
        "hidden": (tp_n, 2, 2 * rows, hid),
        "relay": (2, 2 * rows, hid),
        "passed": (2, 2 * rows, hid),
        "arrived": (2, 2, 2 * rows, hid),
        "wide": (tp_n, 2, 2 * rows, hid),
        "row_grad": (2, 2, rows, feat),
        "returned": (2, 2, rows, feat),
    }
    return {name: pltpu.VMEM((GROUPS,) + shape, BF16) for name, shape in shapes.items()}


def on_device(grad_out, routes, gate_weights, gate_act, w_down, w_up):
    token_n, feat = grad_out.shape
    act, down, up = gate_act[0], w_down[0], w_up[0]
    hid_n = down.shape[0]
    hid = act.shape[1]
    tp_n = hid_n // hid
    piece = token_n // PIECES
    chunks = 2 * GROUPS
    dma = pltpu.SemaphoreType.DMA
    vmem = pl.BlockSpec(memory_space=pltpu.VMEM)
    hbm = pl.BlockSpec(memory_space=pl.ANY)
    return pl.pallas_call(
        on_core,
        out_shape=jax.ShapeDtypeStruct((token_n, feat), BF16),
        in_specs=[vmem, vmem, vmem, hbm, hbm, hbm],
        out_specs=vmem,
        scratch_shapes=[
            pltpu.VMEM(act.shape, BF16),
            pltpu.VMEM(down.shape, BF16),
            pltpu.VMEM(up.shape, BF16),
            pltpu.VMEM((RING, 32, token_n), F32),
            pltpu.VMEM((RING, 32, token_n), F32),
            pltpu.VMEM((RING, token_n, feat), BF16),
            pltpu.VMEM((RING, token_n, feat), F32),
            pltpu.VMEM((2, PIECES, 4, piece, feat), BF16),
            pltpu.VMEM((2, PIECES, 4, piece, feat), BF16),
            [scratch_of(wave, token_n, feat, hid, tp_n) for wave in WAVES],
            dma((3,)),
            dma((8 * PIECES,)), dma((8 * PIECES,)),
            dma((RING,)), dma((RING,)),
            dma((chunks, 2, 2)), dma((chunks, 2, 2)),
            dma((chunks, 4)), dma((chunks, 4)),
            dma((chunks, 2)), dma((chunks, 2)),
            dma((chunks, 2)), dma((chunks, 2)),
            dma((chunks, 2)), dma((chunks, 2)),
            dma((chunks, 2, 2)), dma((chunks, 2, 2)),
            dma((8 * PIECES,)), dma((8 * PIECES,)),
        ],
        compiler_params=pltpu.CompilerParams(
            collective_id=0, has_side_effects=True, vmem_limit_bytes=60 * 1024 * 1024
        ),
    )(grad_out, routes.T, gate_weights.T, act, down, up)


def solution(mesh):
    placed = (
        P("ep", "tp"),
        P("ep", None),
        P("ep", None),
        P("ep", None, "tp"),
        P("ep", None, "tp"),
        P("ep", "tp", None),
    )
    return jax.shard_map(
        on_device, mesh=mesh, in_specs=placed, out_specs=P("ep", "tp"), check_vma=False
    )
```

```python
import functools

import jax
import jax.numpy as jnp
from jax import lax
from jax.experimental import pallas as pl
from jax.experimental.pallas import tpu as pltpu
from jax.sharding import PartitionSpec as P

MESH = pl.DeviceIdType.MESH
RING = 8
SLOT = 10
GROUPS = 4
HOPS = (1, 7, 3, 5, 0, 4, 2, 6)
HOP_CODE = sum(hop << (3 * i) for i, hop in enumerate(HOPS))
EARLY = 2
PIECES = 4
WAVES = ((0, 48, 0, 5), (48, 32, 4, 4))
NEAR = (0, 1, 7, 2, 6, 3, 5, 4)
PLACE = {offset: place for place, offset in enumerate(NEAR)}
COMBINE_LAG = 6
BF16 = jnp.bfloat16
F32 = jnp.float32
ABT = (((1,), (1,)), ((), ()))
ATB = (((0,), (0,)), ((), ()))


def hop_at(i):
    return (HOP_CODE >> (3 * i)) & 7


def pair_of(w, i):
    return i if w == 0 else lax.rem(i + 1, GROUPS)


def hop_of(w, i, kk):
    return hop_at(2 * pair_of(w, i) + kk)


def on_core(
    grad_ref, ids_ref, gates_ref, act_hbm, down_hbm, up_hbm, out_ref,
    act, down, up, meta_out, meta, tokens, totals, sum_out, sum_in, waves,
    load_sem, a_send, a_recv, m_send, m_recv, b_send, b_recv, r_send, r_recv,
    p_send, p_recv, g_send, g_recv, f_send, f_recv, y_send, y_recv, s_send, s_recv,
):
    token_n, feat = grad_ref.shape
    piece = token_n // PIECES
    ep, tp = lax.axis_index("ep"), lax.axis_index("tp")
    tp_n = lax.axis_size("tp")
    core = lax.rem(ep, 2)
    y = lax.rem(ep // 2, RING)
    z = ep // (2 * RING)
    a = z * (1 - core) + y * core
    b = y * (1 - core) + z * core

    def device(a_at, b_at, role, core_at):
        return (a_at * (RING - (RING - 1) * role) + b_at * (1 + (RING - 1) * role)) * 2 + core_at

    def ring(value):
        return lax.rem(value + 2 * RING, RING)

    right, left = lax.rem(tp + 1, tp_n), lax.rem(tp + tp_n - 1, tp_n)
    across = lax.rem(tp + 2, tp_n)

    barrier = pltpu.get_barrier_semaphore()
    for other in range(2):
        for step in range(RING):
            for z_at, y_at in ((ring(z + step), y), (z, ring(y + step)))[: 1 if step == 0 else 2]:
                peer = (z_at * RING + y_at) * 2 + lax.rem(core + other, 2)
                if step or other:
                    pl.semaphore_signal(barrier, inc=1, device_id=(peer, tp), device_id_type=MESH)
    for peer in (right, left):
        pl.semaphore_signal(barrier, inc=1, device_id=(ep, peer), device_id_type=MESH)

    loads = [
        pltpu.make_async_copy(src, dst, load_sem.at[i])
        for i, (src, dst) in enumerate(((act_hbm, act), (down_hbm, down), (up_hbm, up)))
    ]
    for load in loads:
        load.start()

    def remote(src, dst, send, recv, to):
        return pltpu.make_async_remote_copy(
            src_ref=src, dst_ref=dst, send_sem=send, recv_sem=recv, device_id=to, device_id_type=MESH
        )

    def arrival(ref, sem):
        pltpu.make_async_copy(ref, ref, sem).wait()

    pl.semaphore_wait(barrier, 4 * (RING - 1) + 1 + 2)

    a_next = (device(ring(a + 1), b, core, core), device(ring(a - 1), b, core, core))

    def steps_of(way, p):
        return 4 if (p < PIECES // 2) == (way == 0) else 3

    turns = [
        (way, (i + way * PIECES // 2) % PIECES) for i in range(PIECES) for way in range(2)
    ]

    def spread(way, p, s):
        rows = pl.ds(p * piece, piece)
        src_off, dst_off = ((RING - s) % RING, RING - 1 - s) if way == 0 else (s, s + 1)
        src = grad_ref.at[rows] if s == 0 else tokens.at[PLACE[src_off], rows]
        at = (way * PIECES + p) * 4 + s
        return remote(
            src, tokens.at[PLACE[dst_off], rows], a_send.at[at], a_recv.at[at], (a_next[way], tp)
        )

    for way, p in turns:
        spread(way, p, 0).start()
    shape = (token_n, token_n)
    row = lax.broadcasted_iota(jnp.int32, shape, 0)
    chunk_of, core_of = (row >> 1) & 7, row & 1
    a_of = (row // 16 + a) & 7
    b_of = (hop_at(chunk_of) + b) & 7
    expert = a_of * (16 - 14 * core) + b_of * (2 + 14 * core) + core_of
    named = jnp.zeros(shape, F32)
    weight = jnp.zeros(shape, F32)
    for k in range(ids_ref.shape[0]):
        hit = expert == ids_ref[k : k + 1, :]
        named = jnp.where(hit, 1.0, named)
        weight = jnp.where(hit, gates_ref[k : k + 1, :], weight)
    before = (row < lax.broadcasted_iota(jnp.int32, shape, 1)).astype(BF16)
    rank = jnp.dot(named.astype(BF16), before, preferred_element_type=F32)
    slot = jnp.where(named > 0.0, rank, -1000.0)
    for m in range(RING):
        meta_out[m, 0:16, :] = slot[m * 16 : (m + 1) * 16, :]
        meta_out[m, 16:32, :] = weight[m * 16 : (m + 1) * 16, :]
    meta[0] = meta_out[0]
    metas = [
        remote(
            meta_out.at[m], meta.at[PLACE[RING - m]], m_send.at[m], m_recv.at[RING - m],
            (device(ring(a + m), b, core, core), tp),
        )
        for m in range(1, RING)
    ]
    for copy in metas:
        copy.start()

    act_n = act.shape[0]

    def order_act(w):
        row0, rows, _, _ = WAVES[w]
        wide_shape = (4 * rows, 128)
        row = lax.broadcasted_iota(jnp.int32, wide_shape, 0)
        lane = lax.broadcasted_iota(jnp.int32, wide_shape, 1)
        later = row >= 2 * rows
        inner = jnp.where(later, row - 2 * rows, row)
        from_one = inner >= rows
        inner = jnp.where(from_one, inner - rows, inner) + row0
        offset = jnp.full(wide_shape, NEAR[0], jnp.int32)
        in_slot = inner
        for place in range(1, RING):
            past = inner >= place * SLOT
            offset = jnp.where(past, NEAR[place], offset)
            in_slot = jnp.where(past, inner - place * SLOT, in_slot)
        base = in_slot + jnp.where(
            from_one,
            ((offset + y) & 7) * (2 * SLOT) + SLOT,
            ((offset + z) & 7) * (2 * SLOT * RING),
        )

        def order(i, carry):
            hop = jnp.where(later, hop_of(w, i, 1), hop_of(w, i, 0))
            natural = base + jnp.where(
                from_one,
                ((z - hop) & 7) * (2 * SLOT * RING),
                ((y - hop) & 7) * (2 * SLOT),
            )
            pick = jnp.concatenate(
                [(lane + j * 128 == natural).astype(F32).astype(BF16) for j in range(act_n // 128)],
                axis=1,
            )
            got = jnp.dot(pick, act[...], preferred_element_type=F32).astype(BF16)
            ordered = waves[w]["act"]
            ordered[i] = got.reshape(ordered.shape[1:])
            return carry

        return order

    order = [order_act(w) for w in range(2)]

    def gather(w, i):
        row0, rows, place0, places = WAVES[w]
        wave = waves[w]
        msg_row = lax.broadcasted_iota(jnp.int32, (rows, token_n), 0).astype(F32) + float(row0)
        gates = []
        for n in range(4):
            at_row = 4 * pair_of(w, i) + n
            gate = jnp.zeros((rows, token_n), F32)
            for p in range(places):
                place = place0 + p
                at = meta[place, pl.ds(at_row, 1), :] + float(place * SLOT)
                hit = msg_row == at
                gate = jnp.where(hit, meta[place, pl.ds(16 + at_row, 1), :], gate)
                wave["picks"][i, n * rows : (n + 1) * rows, p * token_n : (p + 1) * token_n] = (
                    jnp.where(hit, 1.0, 0.0).astype(BF16)
                )
            gates.append(jnp.sum(gate, axis=1, keepdims=True))
        source = tokens[place0 : place0 + places].reshape(places * token_n, feat)
        value = jnp.dot(wave["picks"][i], source, preferred_element_type=F32)
        for n in range(4):
            wave["to_expert"][i, n // 2, n % 2] = (
                value[n * rows : (n + 1) * rows] * gates[n]
            ).astype(BF16)
        g = w * GROUPS + i
        for n in range(4):
            kk, c = n // 2, n % 2
            hop = hop_of(w, i, kk)
            here = jnp.logical_and(hop == 0, core == c)
            src, dst = wave["to_expert"].at[i, kk, c], wave["routed"].at[i, kk, core]

            @pl.when(here)
            def _():
                pltpu.make_async_copy(src, dst, b_recv.at[g, kk, core]).start()

            @pl.when(jnp.logical_not(here))
            def _():
                remote(
                    src, dst, b_send.at[g, kk, c], b_recv.at[g, kk, core],
                    (device(a, ring(b + hop), core, c), tp),
                ).start()

    def spread_step(s):
        for way, p in turns:
            if s < steps_of(way, p):
                spread(way, p, s - 1).wait_recv()
                spread(way, p, s).start()

    def early(i, carry):
        gather(0, i)
        return carry

    tokens[0] = grad_ref[...]
    totals[...] = jnp.zeros(totals.shape, F32)
    loads[0].wait()
    lax.fori_loop(0, 1, order[0], 0)
    spread_step(1)
    lax.fori_loop(1, GROUPS, order[0], 0)
    spread_step(2)
    for m in range(1, RING):
        metas[m - 1].wait_recv()
    lax.fori_loop(0, EARLY, early, 0)
    spread_step(3)
    loads[1].wait()
    loads[2].wait()

    def r_copy(w, i, n):
        hidden, relay, arrived = waves[w]["hidden"], waves[w]["relay"], waves[w]["arrived"]
        src, dst, to = (
            (hidden.at[i, across, 0], relay.at[i, 0], right),
            (hidden.at[i, right, 1], arrived.at[i, 0, 1], right),
            (hidden.at[i, across, 1], relay.at[i, 1], left),
            (hidden.at[i, left, 0], arrived.at[i, 1, 0], left),
        )[n]
        g = w * GROUPS + i
        return remote(src, dst, r_send.at[g, n], r_recv.at[g, n], (ep, to))

    def p_copy(w, i, way):
        arrived = waves[w]["arrived"]
        dst, to = ((arrived.at[i, 0, 0], right), (arrived.at[i, 1, 1], left))[way]
        g = w * GROUPS + i
        return remote(
            waves[w]["passed"].at[i, way], dst, p_send.at[g, way], p_recv.at[g, way], (ep, to)
        )

    def g_copy(w, i, way):
        part = waves[w]["wide"].at[i, tp]
        g = w * GROUPS + i
        return remote(part, part, g_send.at[g, way], g_recv.at[g, way], (ep, (right, left)[way]))

    def f_copy(w, i, way):
        part = waves[w]["wide"].at[i, (left, right)[way], way]
        g = w * GROUPS + i
        return remote(part, part, f_send.at[g, way], f_recv.at[g, way], (ep, (right, left)[way]))

    def project_down(w, i):
        wave, rows = waves[w], WAVES[w][1]
        for kk in range(2):
            for c in range(2):
                arrival(wave["routed"].at[i, kk, c], b_recv.at[w * GROUPS + i, kk, c])
        got = wave["routed"][i].reshape(4 * rows, feat)
        hidden = wave["hidden"]
        part = hidden.shape[-1]
        for q in range(hidden.shape[1]):
            value = lax.dot_general(
                got, down[q * part : (q + 1) * part, :], ABT, preferred_element_type=F32
            )
            hidden[i, q] = value.astype(BF16).reshape(2, 2 * rows, part)
        for n in (0, 2, 1, 3):
            r_copy(w, i, n).start()

    def pass_on(w, i):
        wave = waves[w]
        for way, to in ((0, right), (1, left)):
            r_copy(w, i, way * 2).wait_recv()
            wave["passed"][i, way] = (
                wave["hidden"][i, to, way].astype(F32) + wave["relay"][i, way].astype(F32)
            ).astype(BF16)
            p_copy(w, i, way).start()

    def finish_hidden(w, i):
        wave = waves[w]
        r_copy(w, i, 1).wait_recv()
        r_copy(w, i, 3).wait_recv()
        p_copy(w, i, 0).wait_recv()
        p_copy(w, i, 1).wait_recv()
        value = wave["hidden"][i, tp].astype(F32) + (
            wave["arrived"][i, 0].astype(F32) + wave["arrived"][i, 1].astype(F32)
        )
        wave["wide"][i, tp] = (value * wave["act"][i].astype(F32)).astype(BF16)
        for way in range(2):
            g_copy(w, i, way).start()

    def hand_over(w, i):
        for way in range(2):
            arrival(waves[w]["wide"].at[i, (left, right)[way]], g_recv.at[w * GROUPS + i, way])
            f_copy(w, i, way).start()

    def project_up(w, i):
        wave, rows = waves[w], WAVES[w][1]
        wide = wave["wide"]
        g = w * GROUPS + i
        for way in range(2):
            arrival(wide.at[i, across, way], f_recv.at[g, way])
        part = wide.shape[-1]
        got = jnp.concatenate(
            [wide[i, q].reshape(4 * rows, part) for q in range(wide.shape[1])], axis=1
        )
        value = lax.dot_general(got, up[...], ABT, preferred_element_type=F32).astype(BF16)
        wave["row_grad"][i] = value.reshape(2, 2, rows, feat)
        for n in range(4):
            kk, c = n // 2, n % 2
            hop = hop_of(w, i, kk)
            here = jnp.logical_and(hop == 0, core == c)
            to = device(z, ring(y - hop), 0, 0) if c == 0 else device(y, ring(z - hop), 1, 1)
            src, dst = wave["row_grad"].at[i, kk, c], wave["returned"].at[i, kk, core]

            @pl.when(here)
            def _():
                pltpu.make_async_copy(src, dst, y_recv.at[g, kk, core]).start()

            @pl.when(jnp.logical_not(here))
            def _():
                remote(
                    src, dst, y_send.at[g, kk, c], y_recv.at[g, kk, core], (to, tp)
                ).start()

    def combine(w, i):
        _, rows, place0, places = WAVES[w]
        wave = waves[w]
        for kk in range(2):
            for c in range(2):
                arrival(wave["returned"].at[i, kk, c], y_recv.at[w * GROUPS + i, kk, c])
        got = wave["returned"][i].reshape(4 * rows, feat)
        value = lax.dot_general(wave["picks"][i], got, ATB, preferred_element_type=F32)
        totals[place0 : place0 + places] += value.reshape(places, token_n, feat)

    stages = (
        (project_down, 0),
        (pass_on, 1),
        (finish_hidden, 2),
        (hand_over, 3),
        (project_up, 4),
        (combine, COMBINE_LAG),
    )

    def chain_of(way, p):
        chain = (4, 3, 2, 1) if way == 0 else (4, 5, 6, 7)
        return chain[4 - steps_of(way, p) :]

    def sum_copy(way, p, s):
        at = (way * PIECES + p) * 4 + s
        return remote(
            sum_out.at[way, p, s], sum_in.at[way, p, s], s_send.at[at], s_recv.at[at],
            (a_next[way], tp),
        )

    def add_on(offsets):
        for way, p in turns:
            for s, offset in enumerate(chain_of(way, p)):
                if offset in offsets:
                    value = totals[PLACE[offset], p * piece : (p + 1) * piece, :]
                    if s:
                        sum_copy(way, p, s - 1).wait_recv()
                        value = value + sum_in[way, p, s - 1].astype(F32)
                    sum_out[way, p, s] = value.astype(BF16)
                    sum_copy(way, p, s).start()

    last = EARLY + GROUPS

    def turn(t, carry):
        for stage, lag in stages:
            g = t - lag

            @pl.when(jnp.logical_and(g >= 0, g < EARLY))
            def _():
                stage(0, g)

            @pl.when(jnp.logical_and(g >= EARLY, g < last))
            def _():
                stage(1, g - EARLY)

            @pl.when(jnp.logical_and(g >= last, g < 2 * GROUPS))
            def _():
                stage(0, g - GROUPS)

            if lag == 0:

                @pl.when(t == 0)
                def _():
                    for way, p in turns:
                        spread(way, p, steps_of(way, p) - 1).wait_recv()

                @pl.when(t < GROUPS)
                def _():
                    gather(1, t)
                    order[1](t, 0)

                @pl.when(jnp.logical_and(t >= GROUPS, t < 2 * GROUPS - EARLY))
                def _():
                    gather(0, t - GROUPS + EARLY)

        @pl.when(t == last - 1 + COMBINE_LAG)
        def _():
            add_on((4,))

        @pl.when(t == last + COMBINE_LAG)
        def _():
            add_on((3, 5))

        return carry

    lax.fori_loop(0, 2 * GROUPS + COMBINE_LAG, turn, 0)
    add_on((2, 6))
    add_on((1, 7))

    for i in range(PIECES):
        p = (i + PIECES // 2) % PIECES
        value = totals[0, p * piece : (p + 1) * piece, :]
        for way in range(2):
            last = steps_of(way, p) - 1
            sum_copy(way, p, last).wait_recv()
            value = value + sum_in[way, p, last].astype(F32)
        out_ref[p * piece : (p + 1) * piece, :] = value.astype(BF16)

    for copy in metas:
        copy.wait_send()
    for way, p in turns:
        for s in range(steps_of(way, p)):
            spread(way, p, s).wait_send()
            sum_copy(way, p, s).wait_send()

    def drain(i, carry):
        for w in range(2):
            g = w * GROUPS + i
            for kk in range(2):
                hop = hop_of(w, i, kk)
                for c in range(2):

                    @pl.when(jnp.logical_not(jnp.logical_and(hop == 0, core == c)))
                    def _():
                        arrival(waves[w]["to_expert"].at[i, kk, c], b_send.at[g, kk, c])
                        arrival(waves[w]["row_grad"].at[i, kk, c], y_send.at[g, kk, c])

            for n in range(4):
                r_copy(w, i, n).wait_send()
            for way in range(2):
                p_copy(w, i, way).wait_send()
                g_copy(w, i, way).wait_send()
                f_copy(w, i, way).wait_send()
        return carry

    lax.fori_loop(0, GROUPS, drain, 0)


def scratch_of(wave, token_n, feat, hid, tp_n):
    _, rows, _, places = wave
    shapes = {
        "act": (2, 2 * rows, hid),
        "picks": (4 * rows, places * token_n),
        "to_expert": (2, 2, rows, feat),
        "routed": (2, 2, rows, feat),
        "hidden": (tp_n, 2, 2 * rows, hid),
        "relay": (2, 2 * rows, hid),
        "passed": (2, 2 * rows, hid),
        "arrived": (2, 2, 2 * rows, hid),
        "wide": (tp_n, 2, 2 * rows, hid),
        "row_grad": (2, 2, rows, feat),
        "returned": (2, 2, rows, feat),
    }
    return {name: pltpu.VMEM((GROUPS,) + shape, BF16) for name, shape in shapes.items()}


def on_device(grad_out, routes, gate_weights, gate_act, w_down, w_up):
    token_n, feat = grad_out.shape
    act, down, up = gate_act[0], w_down[0], w_up[0]
    hid_n = down.shape[0]
    hid = act.shape[1]
    tp_n = hid_n // hid
    piece = token_n // PIECES
    chunks = 2 * GROUPS
    dma = pltpu.SemaphoreType.DMA
    vmem = pl.BlockSpec(memory_space=pltpu.VMEM)
    hbm = pl.BlockSpec(memory_space=pl.ANY)
    return pl.pallas_call(
        on_core,
        out_shape=jax.ShapeDtypeStruct((token_n, feat), BF16),
        in_specs=[vmem, vmem, vmem, hbm, hbm, hbm],
        out_specs=vmem,
        scratch_shapes=[
            pltpu.VMEM(act.shape, BF16),
            pltpu.VMEM(down.shape, BF16),
            pltpu.VMEM(up.shape, BF16),
            pltpu.VMEM((RING, 32, token_n), F32),
            pltpu.VMEM((RING, 32, token_n), F32),
            pltpu.VMEM((RING, token_n, feat), BF16),
            pltpu.VMEM((RING, token_n, feat), F32),
            pltpu.VMEM((2, PIECES, 4, piece, feat), BF16),
            pltpu.VMEM((2, PIECES, 4, piece, feat), BF16),
            [scratch_of(wave, token_n, feat, hid, tp_n) for wave in WAVES],
            dma((3,)),
            dma((8 * PIECES,)), dma((8 * PIECES,)),
            dma((RING,)), dma((RING,)),
            dma((chunks, 2, 2)), dma((chunks, 2, 2)),
            dma((chunks, 4)), dma((chunks, 4)),
            dma((chunks, 2)), dma((chunks, 2)),
            dma((chunks, 2)), dma((chunks, 2)),
            dma((chunks, 2)), dma((chunks, 2)),
            dma((chunks, 2, 2)), dma((chunks, 2, 2)),
            dma((8 * PIECES,)), dma((8 * PIECES,)),
        ],
        compiler_params=pltpu.CompilerParams(
            collective_id=0, has_side_effects=True, vmem_limit_bytes=60 * 1024 * 1024
        ),
    )(grad_out, routes.T, gate_weights.T, act, down, up)


def solution(mesh):
    placed = (
        P("ep", "tp"),
        P("ep", None),
        P("ep", None),
        P("ep", None, "tp"),
        P("ep", None, "tp"),
        P("ep", "tp", None),
    )
    return jax.shard_map(
        on_device, mesh=mesh, in_specs=placed, out_specs=P("ep", "tp"), check_vma=False
    )
```

```python
import functools

import jax
import jax.numpy as jnp
from jax import lax
from jax.experimental import pallas as pl
from jax.experimental.pallas import tpu as pltpu
from jax.sharding import PartitionSpec as P

MESH = pl.DeviceIdType.MESH
RING = 8
SLOT = 10
GROUPS = 4
HOPS = (1, 7, 0, 4, 3, 5, 2, 6)
HOP_CODE = sum(hop << (3 * i) for i, hop in enumerate(HOPS))
EARLY = 2
PIECES = 4
WAVES = ((0, 48, 0, 5), (48, 32, 4, 4))
NEAR = (0, 1, 7, 2, 6, 3, 5, 4)
PLACE = {offset: place for place, offset in enumerate(NEAR)}
COMBINE_LAG = 6
BF16 = jnp.bfloat16
F32 = jnp.float32
ABT = (((1,), (1,)), ((), ()))
ATB = (((0,), (0,)), ((), ()))


def hop_at(i):
    return (HOP_CODE >> (3 * i)) & 7


def pair_of(w, i):
    return i


def hop_of(w, i, kk):
    return hop_at(2 * pair_of(w, i) + kk)


def on_core(
    grad_ref, ids_ref, gates_ref, act_hbm, down_hbm, up_hbm, out_ref,
    act, down, up, meta_out, meta, tokens, totals, sum_out, sum_in, waves,
    load_sem, a_send, a_recv, m_send, m_recv, b_send, b_recv, r_send, r_recv,
    p_send, p_recv, g_send, g_recv, f_send, f_recv, y_send, y_recv, s_send, s_recv,
):
    token_n, feat = grad_ref.shape
    piece = token_n // PIECES
    ep, tp = lax.axis_index("ep"), lax.axis_index("tp")
    tp_n = lax.axis_size("tp")
    core = lax.rem(ep, 2)
    y = lax.rem(ep // 2, RING)
    z = ep // (2 * RING)
    a = z * (1 - core) + y * core
    b = y * (1 - core) + z * core

    def device(a_at, b_at, role, core_at):
        return (a_at * (RING - (RING - 1) * role) + b_at * (1 + (RING - 1) * role)) * 2 + core_at

    def ring(value):
        return lax.rem(value + 2 * RING, RING)

    right, left = lax.rem(tp + 1, tp_n), lax.rem(tp + tp_n - 1, tp_n)
    across = lax.rem(tp + 2, tp_n)

    barrier = pltpu.get_barrier_semaphore()
    for other in range(2):
        for step in range(RING):
            for z_at, y_at in ((ring(z + step), y), (z, ring(y + step)))[: 1 if step == 0 else 2]:
                peer = (z_at * RING + y_at) * 2 + lax.rem(core + other, 2)
                if step or other:
                    pl.semaphore_signal(barrier, inc=1, device_id=(peer, tp), device_id_type=MESH)
    for peer in (right, left):
        pl.semaphore_signal(barrier, inc=1, device_id=(ep, peer), device_id_type=MESH)

    loads = [
        pltpu.make_async_copy(src, dst, load_sem.at[i])
        for i, (src, dst) in enumerate(((act_hbm, act), (down_hbm, down), (up_hbm, up)))
    ]
    for load in loads:
        load.start()

    def remote(src, dst, send, recv, to):
        return pltpu.make_async_remote_copy(
            src_ref=src, dst_ref=dst, send_sem=send, recv_sem=recv, device_id=to, device_id_type=MESH
        )

    def arrival(ref, sem):
        pltpu.make_async_copy(ref, ref, sem).wait()

    pl.semaphore_wait(barrier, 4 * (RING - 1) + 1 + 2)

    a_next = (device(ring(a + 1), b, core, core), device(ring(a - 1), b, core, core))

    def steps_of(way, p):
        return 4 if (p < PIECES // 2) == (way == 0) else 3

    turns = [
        (way, (i + way * PIECES // 2) % PIECES) for i in range(PIECES) for way in range(2)
    ]

    def spread(way, p, s):
        rows = pl.ds(p * piece, piece)
        src_off, dst_off = ((RING - s) % RING, RING - 1 - s) if way == 0 else (s, s + 1)
        src = grad_ref.at[rows] if s == 0 else tokens.at[PLACE[src_off], rows]
        at = (way * PIECES + p) * 4 + s
        return remote(
            src, tokens.at[PLACE[dst_off], rows], a_send.at[at], a_recv.at[at], (a_next[way], tp)
        )

    for way, p in turns:
        spread(way, p, 0).start()
    shape = (token_n, token_n)
    row = lax.broadcasted_iota(jnp.int32, shape, 0)
    chunk_of, core_of = (row >> 1) & 7, row & 1
    a_of = (row // 16 + a) & 7
    b_of = (hop_at(chunk_of) + b) & 7
    expert = a_of * (16 - 14 * core) + b_of * (2 + 14 * core) + core_of
    named = jnp.zeros(shape, F32)
    weight = jnp.zeros(shape, F32)
    for k in range(ids_ref.shape[0]):
        hit = expert == ids_ref[k : k + 1, :]
        named = jnp.where(hit, 1.0, named)
        weight = jnp.where(hit, gates_ref[k : k + 1, :], weight)
    before = (row < lax.broadcasted_iota(jnp.int32, shape, 1)).astype(BF16)
    rank = jnp.dot(named.astype(BF16), before, preferred_element_type=F32)
    slot = jnp.where(named > 0.0, rank, -1000.0)
    for m in range(RING):
        meta_out[m, 0:16, :] = slot[m * 16 : (m + 1) * 16, :]
        meta_out[m, 16:32, :] = weight[m * 16 : (m + 1) * 16, :]
    meta[0] = meta_out[0]
    metas = [
        remote(
            meta_out.at[m], meta.at[PLACE[RING - m]], m_send.at[m], m_recv.at[RING - m],
            (device(ring(a + m), b, core, core), tp),
        )
        for m in range(1, RING)
    ]
    for copy in metas:
        copy.start()

    act_n = act.shape[0]

    def order_act(w):
        row0, rows, _, _ = WAVES[w]
        wide_shape = (4 * rows, 128)
        row = lax.broadcasted_iota(jnp.int32, wide_shape, 0)
        lane = lax.broadcasted_iota(jnp.int32, wide_shape, 1)
        later = row >= 2 * rows
        inner = jnp.where(later, row - 2 * rows, row)
        from_one = inner >= rows
        inner = jnp.where(from_one, inner - rows, inner) + row0
        offset = jnp.full(wide_shape, NEAR[0], jnp.int32)
        in_slot = inner
        for place in range(1, RING):
            past = inner >= place * SLOT
            offset = jnp.where(past, NEAR[place], offset)
            in_slot = jnp.where(past, inner - place * SLOT, in_slot)
        base = in_slot + jnp.where(
            from_one,
            ((offset + y) & 7) * (2 * SLOT) + SLOT,
            ((offset + z) & 7) * (2 * SLOT * RING),
        )

        def order(i, carry):
            hop = jnp.where(later, hop_of(w, i, 1), hop_of(w, i, 0))
            natural = base + jnp.where(
                from_one,
                ((z - hop) & 7) * (2 * SLOT * RING),
                ((y - hop) & 7) * (2 * SLOT),
            )
            pick = jnp.concatenate(
                [(lane + j * 128 == natural).astype(F32).astype(BF16) for j in range(act_n // 128)],
                axis=1,
            )
            got = jnp.dot(pick, act[...], preferred_element_type=F32).astype(BF16)
            ordered = waves[w]["act"]
            ordered[i] = got.reshape(ordered.shape[1:])
            return carry

        return order

    order = [order_act(w) for w in range(2)]

    def gather(w, i):
        row0, rows, place0, places = WAVES[w]
        wave = waves[w]
        msg_row = lax.broadcasted_iota(jnp.int32, (rows, token_n), 0).astype(F32) + float(row0)
        gates = []
        for n in range(4):
            at_row = 4 * pair_of(w, i) + n
            gate = jnp.zeros((rows, token_n), F32)
            for p in range(places):
                place = place0 + p
                at = meta[place, pl.ds(at_row, 1), :] + float(place * SLOT)
                hit = msg_row == at
                gate = jnp.where(hit, meta[place, pl.ds(16 + at_row, 1), :], gate)
                wave["picks"][i, n * rows : (n + 1) * rows, p * token_n : (p + 1) * token_n] = (
                    jnp.where(hit, 1.0, 0.0).astype(BF16)
                )
            gates.append(jnp.sum(gate, axis=1, keepdims=True))
        source = tokens[place0 : place0 + places].reshape(places * token_n, feat)
        value = jnp.dot(wave["picks"][i], source, preferred_element_type=F32)
        for n in range(4):
            wave["to_expert"][i, n // 2, n % 2] = (
                value[n * rows : (n + 1) * rows] * gates[n]
            ).astype(BF16)
        g = w * GROUPS + i
        for n in range(4):
            kk, c = n // 2, n % 2
            hop = hop_of(w, i, kk)
            here = jnp.logical_and(hop == 0, core == c)
            src, dst = wave["to_expert"].at[i, kk, c], wave["routed"].at[i, kk, core]

            @pl.when(here)
            def _():
                pltpu.make_async_copy(src, dst, b_recv.at[g, kk, core]).start()

            @pl.when(jnp.logical_not(here))
            def _():
                remote(
                    src, dst, b_send.at[g, kk, c], b_recv.at[g, kk, core],
                    (device(a, ring(b + hop), core, c), tp),
                ).start()

    def spread_step(s):
        for way, p in turns:
            if s < steps_of(way, p):
                spread(way, p, s - 1).wait_recv()
                spread(way, p, s).start()

    def early(i, carry):
        gather(0, i)
        return carry

    tokens[0] = grad_ref[...]
    totals[...] = jnp.zeros(totals.shape, F32)
    loads[0].wait()
    lax.fori_loop(0, 1, order[0], 0)
    spread_step(1)
    lax.fori_loop(1, GROUPS, order[0], 0)
    spread_step(2)
    for m in range(1, RING):
        metas[m - 1].wait_recv()
    lax.fori_loop(0, EARLY, early, 0)
    spread_step(3)
    loads[1].wait()
    loads[2].wait()

    def r_copy(w, i, n):
        hidden, relay, arrived = waves[w]["hidden"], waves[w]["relay"], waves[w]["arrived"]
        src, dst, to = (
            (hidden.at[i, across, 0], relay.at[i, 0], right),
            (hidden.at[i, right, 1], arrived.at[i, 0, 1], right),
            (hidden.at[i, across, 1], relay.at[i, 1], left),
            (hidden.at[i, left, 0], arrived.at[i, 1, 0], left),
        )[n]
        g = w * GROUPS + i
        return remote(src, dst, r_send.at[g, n], r_recv.at[g, n], (ep, to))

    def p_copy(w, i, way):
        arrived = waves[w]["arrived"]
        dst, to = ((arrived.at[i, 0, 0], right), (arrived.at[i, 1, 1], left))[way]
        g = w * GROUPS + i
        return remote(
            waves[w]["passed"].at[i, way], dst, p_send.at[g, way], p_recv.at[g, way], (ep, to)
        )

    def g_copy(w, i, way):
        part = waves[w]["wide"].at[i, tp]
        g = w * GROUPS + i
        return remote(part, part, g_send.at[g, way], g_recv.at[g, way], (ep, (right, left)[way]))

    def f_copy(w, i, way):
        part = waves[w]["wide"].at[i, (left, right)[way], way]
        g = w * GROUPS + i
        return remote(part, part, f_send.at[g, way], f_recv.at[g, way], (ep, (right, left)[way]))

    def project_down(w, i):
        wave, rows = waves[w], WAVES[w][1]
        for kk in range(2):
            for c in range(2):
                arrival(wave["routed"].at[i, kk, c], b_recv.at[w * GROUPS + i, kk, c])
        got = wave["routed"][i].reshape(4 * rows, feat)
        hidden = wave["hidden"]
        part = hidden.shape[-1]
        for q in range(hidden.shape[1]):
            value = lax.dot_general(
                got, down[q * part : (q + 1) * part, :], ABT, preferred_element_type=F32
            )
            hidden[i, q] = value.astype(BF16).reshape(2, 2 * rows, part)
        for n in (0, 2, 1, 3):
            r_copy(w, i, n).start()

    def pass_on(w, i):
        wave = waves[w]
        for way, to in ((0, right), (1, left)):
            r_copy(w, i, way * 2).wait_recv()
            wave["passed"][i, way] = (
                wave["hidden"][i, to, way].astype(F32) + wave["relay"][i, way].astype(F32)
            ).astype(BF16)
            p_copy(w, i, way).start()

    def finish_hidden(w, i):
        wave = waves[w]
        r_copy(w, i, 1).wait_recv()
        r_copy(w, i, 3).wait_recv()
        p_copy(w, i, 0).wait_recv()
        p_copy(w, i, 1).wait_recv()
        value = wave["hidden"][i, tp].astype(F32) + (
            wave["arrived"][i, 0].astype(F32) + wave["arrived"][i, 1].astype(F32)
        )
        wave["wide"][i, tp] = (value * wave["act"][i].astype(F32)).astype(BF16)
        for way in range(2):
            g_copy(w, i, way).start()

    def hand_over(w, i):
        for way in range(2):
            arrival(waves[w]["wide"].at[i, (left, right)[way]], g_recv.at[w * GROUPS + i, way])
            f_copy(w, i, way).start()

    def project_up(w, i):
        wave, rows = waves[w], WAVES[w][1]
        wide = wave["wide"]
        g = w * GROUPS + i
        for way in range(2):
            arrival(wide.at[i, across, way], f_recv.at[g, way])
        part = wide.shape[-1]
        got = jnp.concatenate(
            [wide[i, q].reshape(4 * rows, part) for q in range(wide.shape[1])], axis=1
        )
        value = lax.dot_general(got, up[...], ABT, preferred_element_type=F32).astype(BF16)
        wave["row_grad"][i] = value.reshape(2, 2, rows, feat)
        for n in range(4):
            kk, c = n // 2, n % 2
            hop = hop_of(w, i, kk)
            here = jnp.logical_and(hop == 0, core == c)
            to = device(z, ring(y - hop), 0, 0) if c == 0 else device(y, ring(z - hop), 1, 1)
            src, dst = wave["row_grad"].at[i, kk, c], wave["returned"].at[i, kk, core]

            @pl.when(here)
            def _():
                pltpu.make_async_copy(src, dst, y_recv.at[g, kk, core]).start()

            @pl.when(jnp.logical_not(here))
            def _():
                remote(
                    src, dst, y_send.at[g, kk, c], y_recv.at[g, kk, core], (to, tp)
                ).start()

    def combine(w, i):
        _, rows, place0, places = WAVES[w]
        wave = waves[w]
        for kk in range(2):
            for c in range(2):
                arrival(wave["returned"].at[i, kk, c], y_recv.at[w * GROUPS + i, kk, c])
        got = wave["returned"][i].reshape(4 * rows, feat)
        value = lax.dot_general(wave["picks"][i], got, ATB, preferred_element_type=F32)
        totals[place0 : place0 + places] += value.reshape(places, token_n, feat)

    stages = (
        (project_down, 0),
        (pass_on, 1),
        (finish_hidden, 2),
        (hand_over, 3),
        (project_up, 4),
        (combine, COMBINE_LAG),
    )

    def chain_of(way, p):
        chain = (4, 3, 2, 1) if way == 0 else (4, 5, 6, 7)
        return chain[4 - steps_of(way, p) :]

    def sum_copy(way, p, s):
        at = (way * PIECES + p) * 4 + s
        return remote(
            sum_out.at[way, p, s], sum_in.at[way, p, s], s_send.at[at], s_recv.at[at],
            (a_next[way], tp),
        )

    def add_on(offsets):
        for way, p in turns:
            for s, offset in enumerate(chain_of(way, p)):
                if offset in offsets:
                    value = totals[PLACE[offset], p * piece : (p + 1) * piece, :]
                    if s:
                        sum_copy(way, p, s - 1).wait_recv()
                        value = value + sum_in[way, p, s - 1].astype(F32)
                    sum_out[way, p, s] = value.astype(BF16)
                    sum_copy(way, p, s).start()

    last = EARLY + GROUPS

    def turn(t, carry):
        for stage, lag in stages:
            g = t - lag

            @pl.when(jnp.logical_and(g >= 0, g < EARLY))
            def _():
                stage(0, g)

            @pl.when(jnp.logical_and(g >= EARLY, g < last))
            def _():
                stage(1, g - EARLY)

            @pl.when(jnp.logical_and(g >= last, g < 2 * GROUPS))
            def _():
                stage(0, g - GROUPS)

            if lag == 0:

                @pl.when(t == 0)
                def _():
                    for way, p in turns:
                        spread(way, p, steps_of(way, p) - 1).wait_recv()

                @pl.when(t < GROUPS)
                def _():
                    gather(1, t)
                    order[1](t, 0)

                @pl.when(jnp.logical_and(t >= GROUPS, t < 2 * GROUPS - EARLY))
                def _():
                    gather(0, t - GROUPS + EARLY)

        @pl.when(t == last - 1 + COMBINE_LAG)
        def _():
            add_on((4,))

        @pl.when(t == last + COMBINE_LAG)
        def _():
            add_on((3, 5))

        return carry

    lax.fori_loop(0, 2 * GROUPS + COMBINE_LAG, turn, 0)
    add_on((2, 6))
    add_on((1, 7))

    for i in range(PIECES):
        p = (i + PIECES // 2) % PIECES
        value = totals[0, p * piece : (p + 1) * piece, :]
        for way in range(2):
            last = steps_of(way, p) - 1
            sum_copy(way, p, last).wait_recv()
            value = value + sum_in[way, p, last].astype(F32)
        out_ref[p * piece : (p + 1) * piece, :] = value.astype(BF16)

    for copy in metas:
        copy.wait_send()
    for way, p in turns:
        for s in range(steps_of(way, p)):
            spread(way, p, s).wait_send()
            sum_copy(way, p, s).wait_send()

    def drain(i, carry):
        for w in range(2):
            g = w * GROUPS + i
            for kk in range(2):
                hop = hop_of(w, i, kk)
                for c in range(2):

                    @pl.when(jnp.logical_not(jnp.logical_and(hop == 0, core == c)))
                    def _():
                        arrival(waves[w]["to_expert"].at[i, kk, c], b_send.at[g, kk, c])
                        arrival(waves[w]["row_grad"].at[i, kk, c], y_send.at[g, kk, c])

            for n in range(4):
                r_copy(w, i, n).wait_send()
            for way in range(2):
                p_copy(w, i, way).wait_send()
                g_copy(w, i, way).wait_send()
                f_copy(w, i, way).wait_send()
        return carry

    lax.fori_loop(0, GROUPS, drain, 0)


def scratch_of(wave, token_n, feat, hid, tp_n):
    _, rows, _, places = wave
    shapes = {
        "act": (2, 2 * rows, hid),
        "picks": (4 * rows, places * token_n),
        "to_expert": (2, 2, rows, feat),
        "routed": (2, 2, rows, feat),
        "hidden": (tp_n, 2, 2 * rows, hid),
        "relay": (2, 2 * rows, hid),
        "passed": (2, 2 * rows, hid),
        "arrived": (2, 2, 2 * rows, hid),
        "wide": (tp_n, 2, 2 * rows, hid),
        "row_grad": (2, 2, rows, feat),
        "returned": (2, 2, rows, feat),
    }
    return {name: pltpu.VMEM((GROUPS,) + shape, BF16) for name, shape in shapes.items()}


def on_device(grad_out, routes, gate_weights, gate_act, w_down, w_up):
    token_n, feat = grad_out.shape
    act, down, up = gate_act[0], w_down[0], w_up[0]
    hid_n = down.shape[0]
    hid = act.shape[1]
    tp_n = hid_n // hid
    piece = token_n // PIECES
    chunks = 2 * GROUPS
    dma = pltpu.SemaphoreType.DMA
    vmem = pl.BlockSpec(memory_space=pltpu.VMEM)
    hbm = pl.BlockSpec(memory_space=pl.ANY)
    return pl.pallas_call(
        on_core,
        out_shape=jax.ShapeDtypeStruct((token_n, feat), BF16),
        in_specs=[vmem, vmem, vmem, hbm, hbm, hbm],
        out_specs=vmem,
        scratch_shapes=[
            pltpu.VMEM(act.shape, BF16),
            pltpu.VMEM(down.shape, BF16),
            pltpu.VMEM(up.shape, BF16),
            pltpu.VMEM((RING, 32, token_n), F32),
            pltpu.VMEM((RING, 32, token_n), F32),
            pltpu.VMEM((RING, token_n, feat), BF16),
            pltpu.VMEM((RING, token_n, feat), F32),
            pltpu.VMEM((2, PIECES, 4, piece, feat), BF16),
            pltpu.VMEM((2, PIECES, 4, piece, feat), BF16),
            [scratch_of(wave, token_n, feat, hid, tp_n) for wave in WAVES],
            dma((3,)),
            dma((8 * PIECES,)), dma((8 * PIECES,)),
            dma((RING,)), dma((RING,)),
            dma((chunks, 2, 2)), dma((chunks, 2, 2)),
            dma((chunks, 4)), dma((chunks, 4)),
            dma((chunks, 2)), dma((chunks, 2)),
            dma((chunks, 2)), dma((chunks, 2)),
            dma((chunks, 2)), dma((chunks, 2)),
            dma((chunks, 2, 2)), dma((chunks, 2, 2)),
            dma((8 * PIECES,)), dma((8 * PIECES,)),
        ],
        compiler_params=pltpu.CompilerParams(
            collective_id=0, has_side_effects=True, vmem_limit_bytes=60 * 1024 * 1024
        ),
    )(grad_out, routes.T, gate_weights.T, act, down, up)


def solution(mesh):
    placed = (
        P("ep", "tp"),
        P("ep", None),
        P("ep", None),
        P("ep", None, "tp"),
        P("ep", None, "tp"),
        P("ep", "tp", None),
    )
    return jax.shard_map(
        on_device, mesh=mesh, in_specs=placed, out_specs=P("ep", "tp"), check_vma=False
    )
```

```python
import functools

import jax
import jax.numpy as jnp
from jax import lax
from jax.experimental import pallas as pl
from jax.experimental.pallas import tpu as pltpu
from jax.sharding import PartitionSpec as P

MESH = pl.DeviceIdType.MESH
RING = 8
SLOT = 10
GROUPS = 4
HOPS = (1, 7, 0, 4, 3, 5, 2, 6)
HOP_CODE = sum(hop << (3 * i) for i, hop in enumerate(HOPS))
EARLY = 2
PIECES = 4
WAVES = ((0, 48, 0, 5), (48, 32, 4, 4))
NEAR = (0, 1, 7, 2, 6, 3, 5, 4)
PLACE = {offset: place for place, offset in enumerate(NEAR)}
COMBINE_LAG = 7
BF16 = jnp.bfloat16
F32 = jnp.float32
ABT = (((1,), (1,)), ((), ()))
ATB = (((0,), (0,)), ((), ()))


def hop_at(i):
    return (HOP_CODE >> (3 * i)) & 7


def pair_of(w, i):
    return i


def hop_of(w, i, kk):
    return hop_at(2 * pair_of(w, i) + kk)


def on_core(
    grad_ref, ids_ref, gates_ref, act_hbm, down_hbm, up_hbm, out_ref,
    act, down, up, meta_out, meta, tokens, totals, sum_out, sum_in, waves,
    load_sem, a_send, a_recv, m_send, m_recv, b_send, b_recv, r_send, r_recv,
    p_send, p_recv, g_send, g_recv, f_send, f_recv, y_send, y_recv, s_send, s_recv,
):
    token_n, feat = grad_ref.shape
    piece = token_n // PIECES
    ep, tp = lax.axis_index("ep"), lax.axis_index("tp")
    tp_n = lax.axis_size("tp")
    core = lax.rem(ep, 2)
    y = lax.rem(ep // 2, RING)
    z = ep // (2 * RING)
    a = z * (1 - core) + y * core
    b = y * (1 - core) + z * core

    def device(a_at, b_at, role, core_at):
        return (a_at * (RING - (RING - 1) * role) + b_at * (1 + (RING - 1) * role)) * 2 + core_at

    def ring(value):
        return lax.rem(value + 2 * RING, RING)

    right, left = lax.rem(tp + 1, tp_n), lax.rem(tp + tp_n - 1, tp_n)
    across = lax.rem(tp + 2, tp_n)

    barrier = pltpu.get_barrier_semaphore()
    for other in range(2):
        for step in range(RING):
            for z_at, y_at in ((ring(z + step), y), (z, ring(y + step)))[: 1 if step == 0 else 2]:
                peer = (z_at * RING + y_at) * 2 + lax.rem(core + other, 2)
                if step or other:
                    pl.semaphore_signal(barrier, inc=1, device_id=(peer, tp), device_id_type=MESH)
    for peer in (right, left):
        pl.semaphore_signal(barrier, inc=1, device_id=(ep, peer), device_id_type=MESH)

    loads = [
        pltpu.make_async_copy(src, dst, load_sem.at[i])
        for i, (src, dst) in enumerate(((act_hbm, act), (down_hbm, down), (up_hbm, up)))
    ]
    for load in loads:
        load.start()

    def remote(src, dst, send, recv, to):
        return pltpu.make_async_remote_copy(
            src_ref=src, dst_ref=dst, send_sem=send, recv_sem=recv, device_id=to, device_id_type=MESH
        )

    def arrival(ref, sem):
        pltpu.make_async_copy(ref, ref, sem).wait()

    pl.semaphore_wait(barrier, 4 * (RING - 1) + 1 + 2)

    a_next = (device(ring(a + 1), b, core, core), device(ring(a - 1), b, core, core))

    def steps_of(way, p):
        return 4 if (p < PIECES // 2) == (way == 0) else 3

    turns = [
        (way, (i + way * PIECES // 2) % PIECES) for i in range(PIECES) for way in range(2)
    ]

    def spread(way, p, s):
        rows = pl.ds(p * piece, piece)
        src_off, dst_off = ((RING - s) % RING, RING - 1 - s) if way == 0 else (s, s + 1)
        src = grad_ref.at[rows] if s == 0 else tokens.at[PLACE[src_off], rows]
        at = (way * PIECES + p) * 4 + s
        return remote(
            src, tokens.at[PLACE[dst_off], rows], a_send.at[at], a_recv.at[at], (a_next[way], tp)
        )

    for way, p in turns:
        spread(way, p, 0).start()
    shape = (token_n, token_n)
    row = lax.broadcasted_iota(jnp.int32, shape, 0)
    chunk_of, core_of = (row >> 1) & 7, row & 1
    a_of = (row // 16 + a) & 7
    b_of = (hop_at(chunk_of) + b) & 7
    expert = a_of * (16 - 14 * core) + b_of * (2 + 14 * core) + core_of
    named = jnp.zeros(shape, F32)
    weight = jnp.zeros(shape, F32)
    for k in range(ids_ref.shape[0]):
        hit = expert == ids_ref[k : k + 1, :]
        named = jnp.where(hit, 1.0, named)
        weight = jnp.where(hit, gates_ref[k : k + 1, :], weight)
    before = (row < lax.broadcasted_iota(jnp.int32, shape, 1)).astype(BF16)
    rank = jnp.dot(named.astype(BF16), before, preferred_element_type=F32)
    slot = jnp.where(named > 0.0, rank, -1000.0)
    for m in range(RING):
        meta_out[m, 0:16, :] = slot[m * 16 : (m + 1) * 16, :]
        meta_out[m, 16:32, :] = weight[m * 16 : (m + 1) * 16, :]
    meta[0] = meta_out[0]
    metas = [
        remote(
            meta_out.at[m], meta.at[PLACE[RING - m]], m_send.at[m], m_recv.at[RING - m],
            (device(ring(a + m), b, core, core), tp),
        )
        for m in range(1, RING)
    ]
    for copy in metas:
        copy.start()

    act_n = act.shape[0]

    def order_act(w):
        row0, rows, _, _ = WAVES[w]
        wide_shape = (4 * rows, 128)
        row = lax.broadcasted_iota(jnp.int32, wide_shape, 0)
        lane = lax.broadcasted_iota(jnp.int32, wide_shape, 1)
        later = row >= 2 * rows
        inner = jnp.where(later, row - 2 * rows, row)
        from_one = inner >= rows
        inner = jnp.where(from_one, inner - rows, inner) + row0
        offset = jnp.full(wide_shape, NEAR[0], jnp.int32)
        in_slot = inner
        for place in range(1, RING):
            past = inner >= place * SLOT
            offset = jnp.where(past, NEAR[place], offset)
            in_slot = jnp.where(past, inner - place * SLOT, in_slot)
        base = in_slot + jnp.where(
            from_one,
            ((offset + y) & 7) * (2 * SLOT) + SLOT,
            ((offset + z) & 7) * (2 * SLOT * RING),
        )

        def order(i, carry):
            hop = jnp.where(later, hop_of(w, i, 1), hop_of(w, i, 0))
            natural = base + jnp.where(
                from_one,
                ((z - hop) & 7) * (2 * SLOT * RING),
                ((y - hop) & 7) * (2 * SLOT),
            )
            pick = jnp.concatenate(
                [(lane + j * 128 == natural).astype(F32).astype(BF16) for j in range(act_n // 128)],
                axis=1,
            )
            got = jnp.dot(pick, act[...], preferred_element_type=F32).astype(BF16)
            ordered = waves[w]["act"]
            ordered[i] = got.reshape(ordered.shape[1:])
            return carry

        return order

    order = [order_act(w) for w in range(2)]

    def gather(w, i):
        row0, rows, place0, places = WAVES[w]
        wave = waves[w]
        msg_row = lax.broadcasted_iota(jnp.int32, (rows, token_n), 0).astype(F32) + float(row0)
        gates = []
        for n in range(4):
            at_row = 4 * pair_of(w, i) + n
            gate = jnp.zeros((rows, token_n), F32)
            for p in range(places):
                place = place0 + p
                at = meta[place, pl.ds(at_row, 1), :] + float(place * SLOT)
                hit = msg_row == at
                gate = jnp.where(hit, meta[place, pl.ds(16 + at_row, 1), :], gate)
                wave["picks"][i, n * rows : (n + 1) * rows, p * token_n : (p + 1) * token_n] = (
                    jnp.where(hit, 1.0, 0.0).astype(BF16)
                )
            gates.append(jnp.sum(gate, axis=1, keepdims=True))
        source = tokens[place0 : place0 + places].reshape(places * token_n, feat)
        value = jnp.dot(wave["picks"][i], source, preferred_element_type=F32)
        for n in range(4):
            wave["to_expert"][i, n // 2, n % 2] = (
                value[n * rows : (n + 1) * rows] * gates[n]
            ).astype(BF16)
        g = w * GROUPS + i
        for n in range(4):
            kk, c = n // 2, n % 2
            hop = hop_of(w, i, kk)
            here = jnp.logical_and(hop == 0, core == c)
            src, dst = wave["to_expert"].at[i, kk, c], wave["routed"].at[i, kk, core]

            @pl.when(here)
            def _():
                pltpu.make_async_copy(src, dst, b_recv.at[g, kk, core]).start()

            @pl.when(jnp.logical_not(here))
            def _():
                remote(
                    src, dst, b_send.at[g, kk, c], b_recv.at[g, kk, core],
                    (device(a, ring(b + hop), core, c), tp),
                ).start()

    def spread_step(s):
        for way, p in turns:
            if s < steps_of(way, p):
                spread(way, p, s - 1).wait_recv()
                spread(way, p, s).start()

    def early(i, carry):
        gather(0, i)
        return carry

    tokens[0] = grad_ref[...]
    totals[...] = jnp.zeros(totals.shape, F32)
    loads[0].wait()
    lax.fori_loop(0, 1, order[0], 0)
    spread_step(1)
    lax.fori_loop(1, GROUPS, order[0], 0)
    spread_step(2)
    for m in range(1, RING):
        metas[m - 1].wait_recv()
    lax.fori_loop(0, EARLY, early, 0)
    spread_step(3)
    loads[1].wait()
    loads[2].wait()

    def r_copy(w, i, n):
        hidden, relay, arrived = waves[w]["hidden"], waves[w]["relay"], waves[w]["arrived"]
        src, dst, to = (
            (hidden.at[i, across, 0], relay.at[i, 0], right),
            (hidden.at[i, right, 1], arrived.at[i, 0, 1], right),
            (hidden.at[i, across, 1], relay.at[i, 1], left),
            (hidden.at[i, left, 0], arrived.at[i, 1, 0], left),
        )[n]
        g = w * GROUPS + i
        return remote(src, dst, r_send.at[g, n], r_recv.at[g, n], (ep, to))

    def p_copy(w, i, way):
        arrived = waves[w]["arrived"]
        dst, to = ((arrived.at[i, 0, 0], right), (arrived.at[i, 1, 1], left))[way]
        g = w * GROUPS + i
        return remote(
            waves[w]["passed"].at[i, way], dst, p_send.at[g, way], p_recv.at[g, way], (ep, to)
        )

    def g_copy(w, i, way):
        part = waves[w]["wide"].at[i, tp]
        g = w * GROUPS + i
        return remote(part, part, g_send.at[g, way], g_recv.at[g, way], (ep, (right, left)[way]))

    def f_copy(w, i, way):
        part = waves[w]["wide"].at[i, (left, right)[way], way]
        g = w * GROUPS + i
        return remote(part, part, f_send.at[g, way], f_recv.at[g, way], (ep, (right, left)[way]))

    def project_down(w, i):
        wave, rows = waves[w], WAVES[w][1]
        for kk in range(2):
            for c in range(2):
                arrival(wave["routed"].at[i, kk, c], b_recv.at[w * GROUPS + i, kk, c])
        got = wave["routed"][i].reshape(4 * rows, feat)
        hidden = wave["hidden"]
        part = hidden.shape[-1]
        for q in range(hidden.shape[1]):
            value = lax.dot_general(
                got, down[q * part : (q + 1) * part, :], ABT, preferred_element_type=F32
            )
            hidden[i, q] = value.astype(BF16).reshape(2, 2 * rows, part)
        for n in (0, 2, 1, 3):
            r_copy(w, i, n).start()

    def pass_on(w, i):
        wave = waves[w]
        for way, to in ((0, right), (1, left)):
            r_copy(w, i, way * 2).wait_recv()
            wave["passed"][i, way] = (
                wave["hidden"][i, to, way].astype(F32) + wave["relay"][i, way].astype(F32)
            ).astype(BF16)
            p_copy(w, i, way).start()

    def finish_hidden(w, i):
        wave = waves[w]
        r_copy(w, i, 1).wait_recv()
        r_copy(w, i, 3).wait_recv()
        p_copy(w, i, 0).wait_recv()
        p_copy(w, i, 1).wait_recv()
        value = wave["hidden"][i, tp].astype(F32) + (
            wave["arrived"][i, 0].astype(F32) + wave["arrived"][i, 1].astype(F32)
        )
        wave["wide"][i, tp] = (value * wave["act"][i].astype(F32)).astype(BF16)
        for way in range(2):
            g_copy(w, i, way).start()

    def hand_over(w, i):
        for way in range(2):
            arrival(waves[w]["wide"].at[i, (left, right)[way]], g_recv.at[w * GROUPS + i, way])
            f_copy(w, i, way).start()

    def project_up(w, i):
        wave, rows = waves[w], WAVES[w][1]
        wide = wave["wide"]
        g = w * GROUPS + i
        for way in range(2):
            arrival(wide.at[i, across, way], f_recv.at[g, way])
        part = wide.shape[-1]
        got = jnp.concatenate(
            [wide[i, q].reshape(4 * rows, part) for q in range(wide.shape[1])], axis=1
        )
        value = lax.dot_general(got, up[...], ABT, preferred_element_type=F32).astype(BF16)
        wave["row_grad"][i] = value.reshape(2, 2, rows, feat)
        for n in range(4):
            kk, c = n // 2, n % 2
            hop = hop_of(w, i, kk)
            here = jnp.logical_and(hop == 0, core == c)
            to = device(z, ring(y - hop), 0, 0) if c == 0 else device(y, ring(z - hop), 1, 1)
            src, dst = wave["row_grad"].at[i, kk, c], wave["returned"].at[i, kk, core]

            @pl.when(here)
            def _():
                pltpu.make_async_copy(src, dst, y_recv.at[g, kk, core]).start()

            @pl.when(jnp.logical_not(here))
            def _():
                remote(
                    src, dst, y_send.at[g, kk, c], y_recv.at[g, kk, core], (to, tp)
                ).start()

    def combine(w, i):
        _, rows, place0, places = WAVES[w]
        wave = waves[w]
        for kk in range(2):
            for c in range(2):
                arrival(wave["returned"].at[i, kk, c], y_recv.at[w * GROUPS + i, kk, c])
        got = wave["returned"][i].reshape(4 * rows, feat)
        value = lax.dot_general(wave["picks"][i], got, ATB, preferred_element_type=F32)
        totals[place0 : place0 + places] += value.reshape(places, token_n, feat)

    stages = (
        (project_down, 0),
        (pass_on, 1),
        (finish_hidden, 2),
        (hand_over, 3),
        (project_up, 4),
        (combine, COMBINE_LAG),
    )

    def chain_of(way, p):
        chain = (4, 3, 2, 1) if way == 0 else (4, 5, 6, 7)
        return chain[4 - steps_of(way, p) :]

    def sum_copy(way, p, s):
        at = (way * PIECES + p) * 4 + s
        return remote(
            sum_out.at[way, p, s], sum_in.at[way, p, s], s_send.at[at], s_recv.at[at],
            (a_next[way], tp),
        )

    def add_on(offsets):
        for way, p in turns:
            for s, offset in enumerate(chain_of(way, p)):
                if offset in offsets:
                    value = totals[PLACE[offset], p * piece : (p + 1) * piece, :]
                    if s:
                        sum_copy(way, p, s - 1).wait_recv()
                        value = value + sum_in[way, p, s - 1].astype(F32)
                    sum_out[way, p, s] = value.astype(BF16)
                    sum_copy(way, p, s).start()

    last = EARLY + GROUPS

    def turn(t, carry):
        for stage, lag in stages:
            g = t - lag

            @pl.when(jnp.logical_and(g >= 0, g < EARLY))
            def _():
                stage(0, g)

            @pl.when(jnp.logical_and(g >= EARLY, g < last))
            def _():
                stage(1, g - EARLY)

            @pl.when(jnp.logical_and(g >= last, g < 2 * GROUPS))
            def _():
                stage(0, g - GROUPS)

            if lag == 0:

                @pl.when(t == 0)
                def _():
                    for way, p in turns:
                        spread(way, p, steps_of(way, p) - 1).wait_recv()

                @pl.when(t < GROUPS)
                def _():
                    gather(1, t)
                    order[1](t, 0)

                @pl.when(jnp.logical_and(t >= GROUPS, t < 2 * GROUPS - EARLY))
                def _():
                    gather(0, t - GROUPS + EARLY)

        @pl.when(t == last - 1 + COMBINE_LAG)
        def _():
            add_on((4,))

        @pl.when(t == last + COMBINE_LAG)
        def _():
            add_on((3, 5))

        return carry

    lax.fori_loop(0, 2 * GROUPS + COMBINE_LAG, turn, 0)
    add_on((2, 6))
    add_on((1, 7))

    for i in range(PIECES):
        p = (i + PIECES // 2) % PIECES
        value = totals[0, p * piece : (p + 1) * piece, :]
        for way in range(2):
            last = steps_of(way, p) - 1
            sum_copy(way, p, last).wait_recv()
            value = value + sum_in[way, p, last].astype(F32)
        out_ref[p * piece : (p + 1) * piece, :] = value.astype(BF16)

    for copy in metas:
        copy.wait_send()
    for way, p in turns:
        for s in range(steps_of(way, p)):
            spread(way, p, s).wait_send()
            sum_copy(way, p, s).wait_send()

    def drain(i, carry):
        for w in range(2):
            g = w * GROUPS + i
            for kk in range(2):
                hop = hop_of(w, i, kk)
                for c in range(2):

                    @pl.when(jnp.logical_not(jnp.logical_and(hop == 0, core == c)))
                    def _():
                        arrival(waves[w]["to_expert"].at[i, kk, c], b_send.at[g, kk, c])
                        arrival(waves[w]["row_grad"].at[i, kk, c], y_send.at[g, kk, c])

            for n in range(4):
                r_copy(w, i, n).wait_send()
            for way in range(2):
                p_copy(w, i, way).wait_send()
                g_copy(w, i, way).wait_send()
                f_copy(w, i, way).wait_send()
        return carry

    lax.fori_loop(0, GROUPS, drain, 0)


def scratch_of(wave, token_n, feat, hid, tp_n):
    _, rows, _, places = wave
    shapes = {
        "act": (2, 2 * rows, hid),
        "picks": (4 * rows, places * token_n),
        "to_expert": (2, 2, rows, feat),
        "routed": (2, 2, rows, feat),
        "hidden": (tp_n, 2, 2 * rows, hid),
        "relay": (2, 2 * rows, hid),
        "passed": (2, 2 * rows, hid),
        "arrived": (2, 2, 2 * rows, hid),
        "wide": (tp_n, 2, 2 * rows, hid),
        "row_grad": (2, 2, rows, feat),
        "returned": (2, 2, rows, feat),
    }
    return {name: pltpu.VMEM((GROUPS,) + shape, BF16) for name, shape in shapes.items()}


def on_device(grad_out, routes, gate_weights, gate_act, w_down, w_up):
    token_n, feat = grad_out.shape
    act, down, up = gate_act[0], w_down[0], w_up[0]
    hid_n = down.shape[0]
    hid = act.shape[1]
    tp_n = hid_n // hid
    piece = token_n // PIECES
    chunks = 2 * GROUPS
    dma = pltpu.SemaphoreType.DMA
    vmem = pl.BlockSpec(memory_space=pltpu.VMEM)
    hbm = pl.BlockSpec(memory_space=pl.ANY)
    return pl.pallas_call(
        on_core,
        out_shape=jax.ShapeDtypeStruct((token_n, feat), BF16),
        in_specs=[vmem, vmem, vmem, hbm, hbm, hbm],
        out_specs=vmem,
        scratch_shapes=[
            pltpu.VMEM(act.shape, BF16),
            pltpu.VMEM(down.shape, BF16),
            pltpu.VMEM(up.shape, BF16),
            pltpu.VMEM((RING, 32, token_n), F32),
            pltpu.VMEM((RING, 32, token_n), F32),
            pltpu.VMEM((RING, token_n, feat), BF16),
            pltpu.VMEM((RING, token_n, feat), F32),
            pltpu.VMEM((2, PIECES, 4, piece, feat), BF16),
            pltpu.VMEM((2, PIECES, 4, piece, feat), BF16),
            [scratch_of(wave, token_n, feat, hid, tp_n) for wave in WAVES],
            dma((3,)),
            dma((8 * PIECES,)), dma((8 * PIECES,)),
            dma((RING,)), dma((RING,)),
            dma((chunks, 2, 2)), dma((chunks, 2, 2)),
            dma((chunks, 4)), dma((chunks, 4)),
            dma((chunks, 2)), dma((chunks, 2)),
            dma((chunks, 2)), dma((chunks, 2)),
            dma((chunks, 2)), dma((chunks, 2)),
            dma((chunks, 2, 2)), dma((chunks, 2, 2)),
            dma((8 * PIECES,)), dma((8 * PIECES,)),
        ],
        compiler_params=pltpu.CompilerParams(
            collective_id=0, has_side_effects=True, vmem_limit_bytes=60 * 1024 * 1024
        ),
    )(grad_out, routes.T, gate_weights.T, act, down, up)


def solution(mesh):
    placed = (
        P("ep", "tp"),
        P("ep", None),
        P("ep", None),
        P("ep", None, "tp"),
        P("ep", None, "tp"),
        P("ep", "tp", None),
    )
    return jax.shard_map(
        on_device, mesh=mesh, in_specs=placed, out_specs=P("ep", "tp"), check_vma=False
    )
```
